256 devices in a mesh: segment: 4 (over y), mp: 16 (over z, core), dp: 4 (over x).
Axes of the slice: x: 4, y: 4, z: 8, core: 2. Of those that a mesh axis runs over, the one named last changes fastest.
Arguments:
- text_rows: bfloat16 [4, 512, 1024], P(None, 'dp'), may hold values from -6 to 6
- durations: int32 [4, 4, 128], P(None, 'dp'), may hold values from 1 to 16, 512 in all within a row
- unit_targets: int32 [4, 2048], P(None, 'dp'), may hold values from 0 to 9999
- w_in: bfloat16 [4, 1024, 8192], P('segment', None, 'mp'), may hold values from -0.1875 to 0.1875
- w_out: bfloat16 [4, 8192, 1024], P('segment', 'mp'), may hold values from -0.0625 to 0.0625
- w_unit: bfloat16 [1024, 10240], P(None, ('segment', 'mp')), as said below
Outputs:
- loss: float32 [4], P('dp')
- grad_in: float32 [4, 1024, 8192], P('segment', 'dp', 'mp')
- grad_out: float32 [4, 8192, 1024], P('segment', 'mp', 'dp')
- grad_unit: float32 [1024, 10240], P('dp', ('segment', 'mp'))
The draws below stay inside these ranges and needn't reach their ends.
Inputs may be any that keep to these rules, and one draw needn't show every extreme that they name: Within each micro-batch and each index of dp the 128 durations sum to exactly 512, and one of them equals 16. `w_unit`: entries of order 3 / sqrt(1024) in most columns, some columns much larger.
All inputs are finite; a program needn't handle non-finite values.
Results may differ from the reference program's by a relative error of at most 0.035.
Values may be sent and summed in bfloat16 or wider, within the bound.
A program may use at most 128 MiB of HBM per device.

```python
import math
import jax
import jax.numpy as jnp
import numpy as np
from jax import lax

D = 1024
FF = 8192
V = 10240
MICRO = 4
ROWS_DEV = 128
UNITS_DEV = 512
TEXT = 512
UNITS = 2048
N_SEGMENT = 4
N_DP = 4


def draw_w_unit(key, part):
    key_a = jax.random.fold_in(jax.random.fold_in(key, 7), 0)
    spread = 3.0 / math.sqrt(D)
    values = jax.random.truncated_normal(key_a, -6.0, 6.0, (D, V), jnp.float32) * spread
    return values.astype(jnp.bfloat16)


def touch_ends(array, own_key, smallest, top_value):
    place = [jax.random.randint(jax.random.fold_in(own_key, axis), (), 0, length) for axis, length in enumerate(array.shape)]
    main_axis = array.shape.index(max(array.shape))
    neighbour = place[:main_axis] + [(place[main_axis] + 1) % array.shape[main_axis]] + place[main_axis + 1:]
    return array.at[tuple(place)].set(smallest).at[tuple(neighbour)].set(top_value)


def shard_levels(stream_key, dims, cuts, low, top_value):
    factor_of, own = 1.0, jax.random.fold_in(stream_key, 6)
    for dim, blocks in cuts:
        draws = jnp.exp(jax.random.uniform(jax.random.fold_in(own, dim), (blocks,), jnp.float32, low / len(cuts), top_value / len(cuts)))
        factor_of = factor_of * jnp.repeat(draws, dims[dim] // blocks).reshape([-1 if axis == dim else 1 for axis in range(len(dims))])
    return factor_of


def cumulative_ranks(amount, skew):
    loads = [(1 << 20) // math.isqrt(standing ** skew) + 1 for standing in range(1, amount + 1)]
    scale = 1 + sum(loads) // (1 << 30)
    return np.cumsum(np.array([max(1, weight // scale) for weight in loads]))


def ranked(key, dims, count, lean):
    listing = cumulative_ranks(count, lean)
    ticket = jax.random.randint(jax.random.fold_in(key, 1), dims, 0, int(listing[count - 1]))
    rank = jnp.searchsorted(jnp.asarray(listing, jnp.int32), ticket, side="right")
    return jax.random.permutation(jax.random.fold_in(key, 2), count)[rank].astype(jnp.int32)


def split_up(amount, total, reach, skew):
    loads = [(1 << 20) // math.isqrt(rank ** skew) + 1 for rank in range(2, amount + 1)]
    rest, holding = total - reach - (amount - 1), [1] * (amount - 1)
    while rest > 0:
        movable = [i for i in range(amount - 1) if holding[i] < reach]
        mass, budget = sum([loads[i] for i in movable]), rest
        for i in movable:
            addition = min(reach - holding[i], max(1, budget * loads[i] // mass), rest)
            holding[i] = holding[i] + addition
            rest = rest - addition
    return np.array([reach] + holding)


def uneven_parts(own_key, number_of, total, bound, skew):
    if number_of == 2:
        one = jax.random.randint(own_key, (), max(1, total - bound), min(bound, total - 1) + 1)
        return jnp.stack([one, total - one])
    sizes = jnp.asarray(split_up(number_of, total, bound, skew), jnp.int32)
    pairs = (number_of - 1) // 2
    source_of, sink = sizes[1:1 + 2 * pairs:2], sizes[2:2 + 2 * pairs:2]
    margin = jnp.minimum(source_of - 1, bound - sink)
    shifted = jax.random.randint(jax.random.fold_in(own_key, 1), (pairs,), 0, 1 << 20) % (margin + 1)
    sizes = sizes.at[1:1 + 2 * pairs:2].set(source_of - shifted).at[2:2 + 2 * pairs:2].set(sink + shifted)
    return sizes[jax.random.permutation(jax.random.fold_in(own_key, 2), number_of)]


def centred(key, extent, width, reach, cuts=(), held_as=jnp.bfloat16):
    level = shard_levels(key, extent, cuts, -0.22, 0.18) if cuts else 1.0
    drawn = jax.random.normal(key, extent, jnp.float32) * width * level
    return jnp.minimum(jnp.maximum(drawn, -reach), reach).astype(held_as)


def setup_inputs(seed: int = 0) -> dict:
    streams_of = jax.random.split(jax.random.key(seed), 7)
    text_rows = centred(streams_of[0], (MICRO, TEXT, D), 1.0, 6.0, ((1, 4),))
    durations = jax.vmap(lambda own: uneven_parts(own, ROWS_DEV, UNITS_DEV, 16, 2))(jax.random.split(streams_of[1], MICRO * N_DP)).reshape((MICRO, N_DP, ROWS_DEV)).astype(jnp.int32)
    unit_targets = touch_ends(ranked(streams_of[2], (MICRO, UNITS), min(V, 10000), 2), jax.random.fold_in(streams_of[2], 3), 0, (min(V, 10000)) - 1).astype(jnp.int32)
    w_in = centred(streams_of[3], (N_SEGMENT, D, FF), D ** -0.5, 0.1875, ((0, 4), (2, 16)))
    w_out = centred(streams_of[4], (N_SEGMENT, FF, D), FF ** -0.5, 0.0625, ((0, 4), (1, 16)))
    w_unit = draw_w_unit(jax.random.fold_in(streams_of[6], 71), 0)
    return {"text_rows": text_rows, "durations": durations, "unit_targets": unit_targets, "w_in": w_in, "w_out": w_out, "w_unit": w_unit}


def gelu_parts(pre_vals):
    coeff = 0.7978845608
    inner = coeff * (pre_vals + 0.044715 * pre_vals * pre_vals * pre_vals)
    tanh_val = jnp.tanh(inner)
    value = 0.5 * pre_vals * (1.0 + tanh_val)
    slope = 0.5 * (1.0 + tanh_val) + 0.5 * pre_vals * (1.0 - tanh_val * tanh_val) * coeff * (1.0 + 3.0 * 0.044715 * pre_vals * pre_vals)
    return (value, slope)

def row_scale(rows_in):
    floats = rows_in.astype(jnp.float32)
    return lax.rsqrt(lax.optimization_barrier(jnp.mean(floats * floats, axis=-1, keepdims=True)) + 1e-06)

def norm_back(rows_in, grads):
    scale = row_scale(rows_in)
    normal = rows_in.astype(jnp.float32) * scale
    return scale * (grads - normal * lax.optimization_barrier(jnp.mean(grads * normal, axis=-1, keepdims=True)))

def section(rows_in, first, second):
    normed = (rows_in.astype(jnp.float32) * row_scale(rows_in)).astype(jnp.bfloat16)
    pre_vals = jnp.dot(normed, first, preferred_element_type=jnp.float32)
    value, slope = gelu_parts(pre_vals)
    hidden = value.astype(jnp.bfloat16)
    return (normed, hidden, slope)

def reference(text_rows, durations, unit_targets, w_in, w_out, w_unit):
    total_rows = MICRO * TEXT
    rows_now = text_rows.reshape(total_rows, D)
    stored = []
    for segment_id in range(N_SEGMENT):
        stored.append(rows_now)
        normed, hidden, slope = section(rows_now, w_in[segment_id], w_out[segment_id])
        rows_now = (rows_now.astype(jnp.float32) + jnp.dot(hidden, w_out[segment_id], preferred_element_type=jnp.float32)).astype(jnp.bfloat16)
    final_norm = (rows_now.astype(jnp.float32) * row_scale(rows_now)).astype(jnp.bfloat16)
    logits = jnp.dot(final_norm, w_unit, preferred_element_type=jnp.float32)
    ends = jnp.cumsum(durations, axis=-1)
    positions = jnp.arange(UNITS_DEV, dtype=jnp.int32)
    row_local = lax.optimization_barrier(jnp.sum((ends[:, :, None, :] <= positions[None, None, :, None]).astype(jnp.int32), axis=-1))
    block_ids = jnp.arange(MICRO * N_DP, dtype=jnp.int32).reshape(MICRO, N_DP, 1)
    row_global = (block_ids * ROWS_DEV + row_local).reshape(-1).astype(jnp.int32)
    target_flat = unit_targets.reshape(-1).astype(jnp.int32)
    counts = jnp.zeros((total_rows, V), jnp.float32).at[row_global, target_flat].add(1.0)
    duration_f = durations.reshape(total_rows).astype(jnp.float32)
    peak = lax.optimization_barrier(jnp.max(logits, axis=-1))
    lse = peak + jnp.log(lax.optimization_barrier(jnp.sum(jnp.exp(logits - peak[:, None]), axis=-1)))
    denom = float(MICRO * UNITS)
    loss_terms = duration_f * lse - lax.optimization_barrier(jnp.sum(counts * logits, axis=-1))
    loss = lax.optimization_barrier(jnp.sum(loss_terms.reshape(MICRO, N_DP, ROWS_DEV), axis=(0, 2))) / denom
    dlogits = ((duration_f[:, None] * jnp.exp(logits - lse[:, None]) - counts) / denom).astype(jnp.bfloat16)
    grad_unit = jnp.dot(final_norm.T, dlogits, preferred_element_type=jnp.float32)
    dnorm = jnp.dot(dlogits, w_unit.T, preferred_element_type=jnp.float32).astype(jnp.bfloat16)
    grads = norm_back(rows_now, dnorm.astype(jnp.float32)).astype(jnp.bfloat16)
    grads_in = []
    grads_out = []
    for segment_id in reversed(range(N_SEGMENT)):
        rows_in = stored[segment_id]
        normed, hidden, slope = section(rows_in, w_in[segment_id], w_out[segment_id])
        grads_out.append(jnp.dot(hidden.T, grads, preferred_element_type=jnp.float32))
        dhidden = jnp.dot(grads, w_out[segment_id].T, preferred_element_type=jnp.float32)
        dpre = (dhidden * slope).astype(jnp.bfloat16)
        grads_in.append(jnp.dot(normed.T, dpre, preferred_element_type=jnp.float32))
        dnormed = jnp.dot(dpre, w_in[segment_id].T, preferred_element_type=jnp.float32)
        grads = (grads.astype(jnp.float32) + norm_back(rows_in, dnormed)).astype(jnp.bfloat16)
    grad_in = jnp.stack(grads_in[::-1], axis=0)
    grad_out = jnp.stack(grads_out[::-1], axis=0)
    return (loss, grad_in, grad_out, grad_unit)
```

```python
import jax
import jax.numpy as jnp
from jax import lax
from jax.experimental import pallas as pl
from jax.experimental.pallas import tpu as pltpu
from jax.sharding import PartitionSpec as P

MESH = pl.DeviceIdType.MESH
F32 = jnp.float32
BF16 = jnp.bfloat16

(
    G_FRS, G_FAG, G_FINY, G_FINZ, G_STAT, G_NRS, G_NY, G_NAG, G_BRS, G_BAG, G_TEXT, G_LOSS, G_SIBW,
) = range(13)
N_GROUPS = 13


def gelu_parts(pre_vals):
    coeff = 0.7978845608
    inner = coeff * (pre_vals + 0.044715 * pre_vals * pre_vals * pre_vals)
    tanh_val = jnp.tanh(inner)
    value = 0.5 * pre_vals * (1.0 + tanh_val)
    slope = 0.5 * (1.0 + tanh_val) + 0.5 * pre_vals * (1.0 - tanh_val * tanh_val) * coeff * (
        1.0 + 3.0 * 0.044715 * pre_vals * pre_vals
    )
    return (value, slope)


def row_scale(floats):
    return lax.rsqrt(jnp.mean(floats * floats, axis=-1, keepdims=True) + 1e-06)


def nn(a, b):
    return jnp.dot(a, b, preferred_element_type=F32)


def nt(a, b):
    return lax.dot_general(a, b, (((1,), (1,)), ((), ())), preferred_element_type=F32)


def tn(a, b):
    return lax.dot_general(a, b, (((0,), (0,)), ((), ())), preferred_element_type=F32)


def make_kernel(n_seg, n_z, n_dp, chunks, rows, width, hid_dev, voc_dev, units, denom):
    own_rows = rows // n_z
    n_peer = n_seg * n_z

    def kernel(
        text, dur, tgt, w_in, w_out, w_unit,
        loss_o, gin_o, gout_o, gun_o,
        wi_sib, wo_sib, wu_sib,
        xbuf, normed, part, rsf, osh, hid, slo,
        fin, fn, lg, cnt, stb, dlb, partd, rsd, ysend, yrecv, dxb, dsh,
        dpre, partb, rsb, bsh,
        gs_sib, gr_sib, gi_sib, gir_sib, gu_f, gu_sib, gur_sib, go_f, gi_f,
        xs_u, xr_u, xs_o, xr_o, xs_i, xr_i,
        lvec, lown, lrcv,
        ssem, rsem, sib_s, sib_r, dp_s, dp_r,
    ):
        s = lax.axis_index("segment")
        mp = lax.axis_index("mp")
        d = lax.axis_index("dp")
        z = lax.div(mp, 2)
        c = lax.rem(mp, 2)
        sib = 2 * z + (1 - c)
        me = s * n_z + z

        def rds(k, zz):
            return pl.ds(pl.multiple_of(k * rows + zz * own_rows, own_rows), own_rows)

        def kds(k):
            return pl.ds(pl.multiple_of(k * rows, rows), rows)

        def put(src, dst, a, b, where):
            pltpu.make_async_remote_copy(
                src_ref=src, dst_ref=dst, send_sem=a, recv_sem=b, device_id=where, device_id_type=MESH
            ).start()

        def drain(ref, sem):
            pltpu.make_async_copy(ref, ref, sem).wait()

        def peers_z(fn_of):
            def step(off, carry):
                fn_of(lax.rem(z + off, n_z))
                return carry

            lax.fori_loop(1, n_z, step, 0)

        def over(n, fn_of):
            def step(i, carry):
                fn_of(i)
                return carry

            lax.fori_loop(0, n, step, 0)

        barrier = pltpu.get_barrier_semaphore()

        def hello(off, carry):
            other = lax.rem(me + off, n_peer)
            pl.semaphore_signal(
                barrier, inc=1,
                device_id={"segment": lax.div(other, n_z), "mp": 2 * lax.rem(other, n_z) + c},
                device_id_type=MESH,
            )
            return carry

        lax.fori_loop(1, n_peer, hello, 0)

        def hello_dp(off, carry):
            pl.semaphore_signal(
                barrier, inc=1, device_id={"dp": lax.rem(d + off, n_dp)}, device_id_type=MESH
            )
            return carry

        lax.fori_loop(1, n_dp, hello_dp, 0)
        pl.semaphore_signal(barrier, inc=1, device_id={"mp": sib}, device_id_type=MESH)
        pl.semaphore_wait(barrier, n_peer - 1 + n_dp - 1 + 1)

        put(w_in, wi_sib, ssem.at[G_SIBW, 0], rsem.at[G_SIBW, 0], {"mp": sib})
        put(w_out, wo_sib, ssem.at[G_SIBW, 1], rsem.at[G_SIBW, 1], {"mp": sib})
        put(w_unit, wu_sib, ssem.at[G_LOSS, 1], rsem.at[G_LOSS, 1], {"mp": sib})

        @pl.when(s == 0)
        def _():
            def load(k):
                pltpu.make_async_copy(
                    text.at[chunks * c + k], xbuf.at[kds(k)], rsem.at[G_TEXT, k]
                ).start()

            over(chunks, load)

        def forward(k):
            @pl.when(s == 0)
            def _():
                drain(xbuf.at[kds(k)], rsem.at[G_TEXT, k])

            @pl.when(s > 0)
            def _():
                drain(xbuf.at[kds(k)], rsem.at[G_FAG, k])

            x = xbuf[kds(k), :].astype(F32)
            n = (x * row_scale(x)).astype(BF16)
            normed[kds(k), :] = n

            value, slope = gelu_parts(nn(n, w_in[...]))
            h0 = value.astype(BF16)
            hid[0, kds(k), :] = h0
            slo[0, kds(k), :] = slope
            acc = nn(h0, w_out[...])

            @pl.when(k == 0)
            def _():
                drain(wi_sib, rsem.at[G_SIBW, 0])
                drain(wo_sib, rsem.at[G_SIBW, 1])

            value, slope = gelu_parts(nn(n, wi_sib[...]))
            h1 = value.astype(BF16)
            hid[1, kds(k), :] = h1
            slo[1, kds(k), :] = slope
            acc = acc + nn(h1, wo_sib[...])
            part[kds(k), :] = acc.astype(BF16)
            rsf[k, z] = part[rds(k, z), :]
            peers_z(
                lambda z2: put(
                    part.at[rds(k, z2)], rsf.at[k, z], ssem.at[G_FRS, k], rsem.at[G_FRS, k],
                    {"mp": 2 * z2 + c},
                )
            )

        over(chunks, forward)

        def count(k):
            lengths = dur[chunks * c + k].astype(F32)
            lane = lax.broadcasted_iota(jnp.int32, (rows, rows), 1)
            sub = lax.broadcasted_iota(jnp.int32, (rows, rows), 0)
            tri = jnp.where(sub <= lane, 1.0, 0.0).astype(BF16)
            wide = jnp.broadcast_to(lengths, (8, rows)).astype(BF16)
            ends = nn(wide, tri)[0:1, :]
            starts = ends - lengths
            unit = lax.broadcasted_iota(jnp.int32, (units, rows), 0).astype(F32)
            onehot = jnp.where((starts <= unit) & (unit < ends), 1.0, 0.0).astype(BF16)
            target = tgt[chunks * c + k]
            ids = lax.broadcasted_iota(jnp.int32, (voc_dev, units), 0)
            for h, owner in ((0, mp), (1, sib)):
                first = (s * (2 * n_z) + owner) * voc_dev
                hits = jnp.where(ids + first == target, 1.0, 0.0).astype(BF16)
                cnt[k, h] = nn(hits, onehot)

        over(chunks, count)

        def owned_sum(buf, k):
            total = buf[k, 0].astype(F32)
            for i in range(1, n_z):
                total = total + buf[k, i].astype(F32)
            return total

        def forward_end(k):
            drain(rsf.at[k, pl.ds(0, n_z - 1)], rsem.at[G_FRS, k])
            x = xbuf[rds(k, z), :].astype(F32)
            new = (x + owned_sum(rsf, k)).astype(BF16)
            osh[k] = new

            @pl.when(s < n_seg - 1)
            def _():
                def send(z2):
                    put(
                        osh.at[k], xbuf.at[rds(k, z)], ssem.at[G_FAG, k], rsem.at[G_FAG, k],
                        {"segment": s + 1, "mp": 2 * z2 + c},
                    )

                over(n_z, lambda i: send(lax.rem(z + i, n_z)))

            @pl.when(s == n_seg - 1)
            def _():
                fin[rds(k, z), :] = new

                def send(y2):
                    put(
                        osh.at[k], fin.at[rds(k, z)], ssem.at[G_FINY, k], rsem.at[G_FINY, k],
                        {"segment": y2},
                    )

                over(n_seg - 1, send)

        over(chunks, forward_end)

        def relay(k):
            @pl.when(s < n_seg - 1)
            def _():
                drain(fin.at[rds(k, z)], rsem.at[G_FINY, k])

            peers_z(
                lambda z2: put(
                    fin.at[rds(k, z)], fin.at[rds(k, z)], ssem.at[G_FINZ, k], rsem.at[G_FINZ, k],
                    {"mp": 2 * z2 + c},
                )
            )

        over(chunks, relay)
        drain(wu_sib, rsem.at[G_LOSS, 1])

        def logits(k):
            drain(rsf.at[k, pl.ds(0, n_z - 1)], rsem.at[G_FINZ, k])
            x = fin[kds(k), :].astype(F32)
            n = (x * row_scale(x)).astype(BF16)
            fn[kds(k), :] = n
            a = nt(w_unit[...], n)
            b = nt(wu_sib[...], n)
            lg[k, 0] = a
            lg[k, 1] = b
            peak = jnp.maximum(jnp.max(a, axis=0, keepdims=True), jnp.max(b, axis=0, keepdims=True))
            total = jnp.sum(jnp.exp(a - peak), axis=0, keepdims=True) + jnp.sum(
                jnp.exp(b - peak), axis=0, keepdims=True
            )
            hit = jnp.sum(cnt[k, 0] * a, axis=0, keepdims=True) + jnp.sum(
                cnt[k, 1] * b, axis=0, keepdims=True
            )
            sub = lax.broadcasted_iota(jnp.int32, (8, rows), 0)
            stb[k, me] = jnp.where(sub == 0, peak, jnp.where(sub == 1, total, hit))

            def send(off, carry):
                other = lax.rem(me + off, n_peer)
                put(
                    stb.at[k, me], stb.at[k, me], ssem.at[G_STAT, k], rsem.at[G_STAT, k],
                    {"segment": lax.div(other, n_z), "mp": 2 * lax.rem(other, n_z) + c},
                )
                return carry

            lax.fori_loop(1, n_peer, send, 0)

        over(chunks, logits)

        lvec[...] = jnp.zeros_like(lvec)

        def dlogits(k):
            drain(stb.at[k, pl.ds(0, n_peer - 1)], rsem.at[G_STAT, k])
            every = stb[k]
            peaks = every[:, 0:1, :]
            peak = jnp.max(peaks, axis=0)
            total = jnp.sum(every[:, 1:2, :] * jnp.exp(peaks - peak[None]), axis=0)
            hit = jnp.sum(every[:, 2:3, :], axis=0)
            lse = peak + jnp.log(total)
            lengths = dur[chunks * c + k].astype(F32)
            lvec[0:1, :] += lengths * lse - hit
            acc = None
            for h, w in ((0, w_unit), (1, wu_sib)):
                grad = (lengths * jnp.exp(lg[k, h] - lse) - cnt[k, h]) * (1.0 / denom)
                grad = grad.astype(BF16)
                dlb[h, k] = grad
                term = tn(grad, w[...])
                acc = term if acc is None else acc + term
            partd[kds(k), :] = acc.astype(BF16)
            rsd[k, z] = partd[rds(k, z), :]
            peers_z(
                lambda z2: put(
                    partd.at[rds(k, z2)], rsd.at[k, z], ssem.at[G_NRS, k], rsem.at[G_NRS, k],
                    {"mp": 2 * z2 + c},
                )
            )

        over(chunks, dlogits)

        lown[...] = jnp.broadcast_to(jnp.sum(lvec[...], keepdims=True), lown.shape)
        put(lown, lrcv, ssem.at[G_LOSS, 0], rsem.at[G_LOSS, 0], {"mp": sib})

        quarter = width // n_dp
        for h in (1, 0):
            total = nn(dlb[h, 0], fn[pl.ds(0, rows), :])
            for k in range(1, chunks):
                total = total + nn(dlb[h, k], fn[pl.ds(k * rows, rows), :])
            for q in range(n_dp):
                piece = total[:, q * quarter : (q + 1) * quarter]
                if h == 1:
                    gu_sib[q] = piece.astype(BF16)
                else:
                    gu_f[q] = piece
            if h == 1:
                put(gu_sib, gur_sib, sib_s.at[0], sib_r.at[0], {"mp": sib})

        def norm_sum(k):
            drain(rsd.at[k, pl.ds(0, n_z - 1)], rsem.at[G_NRS, k])
            total = owned_sum(rsd, k)
            ysend[k] = total.astype(BF16)

            @pl.when(s < n_seg - 1)
            def _():
                put(
                    ysend.at[k], yrecv.at[k, s], ssem.at[G_NY, k], rsem.at[G_NY, k],
                    {"segment": n_seg - 1},
                )

        over(chunks, norm_sum)

        @pl.when(s == n_seg - 1)
        def _():
            def norm_end(k):
                drain(yrecv.at[k], rsem.at[G_NY, k])
                total = ysend[k].astype(F32)
                for i in range(n_seg - 1):
                    total = total + yrecv[k, i].astype(F32)
                g = total.astype(BF16).astype(F32)
                x = fin[rds(k, z), :].astype(F32)
                scale = row_scale(x)
                n = x * scale
                grad = scale * (g - n * jnp.mean(g * n, axis=-1, keepdims=True))
                grad = grad.astype(BF16)
                dsh[k] = grad
                dxb[rds(k, z), :] = grad
                peers_z(
                    lambda z2: put(
                        dsh.at[k], dxb.at[rds(k, z)], ssem.at[G_NAG, k], rsem.at[G_NAG, k],
                        {"mp": 2 * z2 + c},
                    )
                )

            over(chunks, norm_end)

        def dp_send(xs, xr, g):
            def step(off, carry):
                d2 = lax.rem(d + off, n_dp)
                put(xs.at[d2], xr.at[d], dp_s.at[g], dp_r.at[g], {"dp": d2})
                return carry

            lax.fori_loop(1, n_dp, step, 0)

        def dp_out(own, xr, g, out):
            drain(xr.at[pl.ds(0, n_dp - 1)], dp_r.at[g])
            total = own
            for off in range(1, n_dp):
                total = total + xr[lax.rem(d + off, n_dp)].astype(F32)
            out[...] = total

        drain(gur_sib, sib_r.at[0])

        def unit_sum(q):
            total = gu_f[q] + gur_sib[q].astype(F32)
            gu_f[q] = total
            xs_u[q] = total.astype(BF16)

        over(n_dp, unit_sum)
        dp_send(xs_u, xr_u, 0)

        def backward(k):
            @pl.when(s == n_seg - 1)
            def _():
                drain(rsf.at[k, pl.ds(0, n_z - 1)], rsem.at[G_NAG, k])

            @pl.when(s < n_seg - 1)
            def _():
                drain(dxb.at[kds(k)], rsem.at[G_BAG, k])

            g = dxb[kds(k), :]
            p0 = (nt(g, w_out[...]) * slo[0, kds(k), :]).astype(BF16)
            dpre[0, kds(k), :] = p0
            p1 = (nt(g, wo_sib[...]) * slo[1, kds(k), :]).astype(BF16)
            dpre[1, kds(k), :] = p1

            @pl.when(s > 0)
            def _():
                partb[kds(k), :] = (nt(p0, w_in[...]) + nt(p1, wi_sib[...])).astype(BF16)
                rsb[k, z] = partb[rds(k, z), :]
                peers_z(
                    lambda z2: put(
                        partb.at[rds(k, z2)], rsb.at[k, z], ssem.at[G_BRS, k], rsem.at[G_BRS, k],
                        {"mp": 2 * z2 + c},
                    )
                )

        over(chunks, backward)

        @pl.when(s > 0)
        def _():
            def backward_end(k):
                drain(rsb.at[k, pl.ds(0, n_z - 1)], rsem.at[G_BRS, k])
                g = owned_sum(rsb, k)
                x = xbuf[rds(k, z), :].astype(F32)
                scale = row_scale(x)
                n = x * scale
                back = scale * (g - n * jnp.mean(g * n, axis=-1, keepdims=True))
                bsh[k] = (dxb[rds(k, z), :].astype(F32) + back).astype(BF16)

                def send(z2):
                    put(
                        bsh.at[k], dxb.at[rds(k, z)], ssem.at[G_BAG, k], rsem.at[G_BAG, k],
                        {"segment": s - 1, "mp": 2 * z2 + c},
                    )

                over(n_z, lambda i: send(lax.rem(z + i, n_z)))

            over(chunks, backward_end)

        out_q = width // n_dp
        for q in range(n_dp):
            gs_sib[q] = tn(hid[1], dxb[:, q * out_q : (q + 1) * out_q]).astype(BF16)
        put(gs_sib, gr_sib, sib_s.at[1], sib_r.at[1], {"mp": sib})
        for q in range(n_dp):
            go_f[q] = tn(hid[0], dxb[:, q * out_q : (q + 1) * out_q])
        for q in range(n_dp):
            gi_sib[q] = tn(normed[:, q * out_q : (q + 1) * out_q], dpre[1]).astype(BF16)
        put(gi_sib, gir_sib, sib_s.at[2], sib_r.at[2], {"mp": sib})
        drain(gr_sib, sib_r.at[1])

        def out_sum(q):
            total = go_f[q] + gr_sib[q].astype(F32)
            go_f[q] = total
            xs_o[q] = total.astype(BF16)

        over(n_dp, out_sum)
        dp_send(xs_o, xr_o, 1)
        for q in range(n_dp):
            gi_f[q] = tn(normed[:, q * out_q : (q + 1) * out_q], dpre[0])
        drain(gir_sib, sib_r.at[2])

        def in_sum(q):
            total = gi_f[q] + gir_sib[q].astype(F32)
            gi_f[q] = total
            xs_i[q] = total.astype(BF16)

        over(n_dp, in_sum)
        dp_send(xs_i, xr_i, 2)

        dp_out(gu_f[d], xr_u, 0, gun_o)
        drain(lrcv, rsem.at[G_LOSS, 0])
        loss_o[...] = (lown[...] + lrcv[...]) * (1.0 / denom)
        dp_out(go_f[d], xr_o, 1, gout_o)
        dp_out(gi_f[d], xr_i, 2, gin_o)

        drain(w_in, ssem.at[G_SIBW, 0])
        drain(w_out, ssem.at[G_SIBW, 1])
        drain(w_unit, ssem.at[G_LOSS, 1])
        drain(lown, ssem.at[G_LOSS, 0])
        drain(gu_sib, sib_s.at[0])
        drain(gs_sib, sib_s.at[1])
        drain(gi_sib, sib_s.at[2])
        drain(xs_u.at[pl.ds(0, n_dp - 1)], dp_s.at[0])
        drain(xs_o.at[pl.ds(0, n_dp - 1)], dp_s.at[1])
        drain(xs_i.at[pl.ds(0, n_dp - 1)], dp_s.at[2])

        def finish(k):
            part_of = rsf.at[k, pl.ds(0, n_z - 1)]
            drain(part_of, ssem.at[G_FRS, k])
            drain(part_of, ssem.at[G_FINZ, k])
            drain(part_of, ssem.at[G_NRS, k])
            drain(stb.at[k, pl.ds(0, n_peer - 1)], ssem.at[G_STAT, k])

            @pl.when(s < n_seg - 1)
            def _():
                drain(rsf.at[k], ssem.at[G_FAG, k])
                drain(ysend.at[k], ssem.at[G_NY, k])

            @pl.when(s == n_seg - 1)
            def _():
                drain(yrecv.at[k], ssem.at[G_FINY, k])
                drain(part_of, ssem.at[G_NAG, k])

            @pl.when(s > 0)
            def _():
                drain(part_of, ssem.at[G_BRS, k])
                drain(rsf.at[k], ssem.at[G_BAG, k])

        over(chunks, finish)

    vm = pltpu.VMEM
    all_rows = chunks * rows
    shard = (chunks, own_rows, width)
    scatter = (chunks, n_z, own_rows, width)
    quarter = width // n_dp
    scratch = [
        vm((width, hid_dev), BF16), vm((hid_dev, width), BF16), vm((voc_dev, width), BF16),
        vm((all_rows, width), BF16), vm((all_rows, width), BF16), vm((all_rows, width), BF16),
        vm(scatter, BF16), vm(shard, BF16), vm((2, all_rows, hid_dev), BF16), vm((2, all_rows, hid_dev), F32),
        vm((all_rows, width), BF16), vm((all_rows, width), BF16),
        vm((chunks, 2, voc_dev, rows), F32), vm((chunks, 2, voc_dev, rows), F32),
        vm((chunks, n_peer, 8, rows), F32), vm((2, chunks, voc_dev, rows), BF16),
        vm((all_rows, width), BF16), vm(scatter, BF16), vm(shard, BF16),
        vm((chunks, n_seg - 1, own_rows, width), BF16), vm((all_rows, width), BF16), vm(shard, BF16),
        vm((2, all_rows, hid_dev), BF16), vm((all_rows, width), BF16), vm(scatter, BF16), vm(shard, BF16),
        vm((n_dp, hid_dev, quarter), BF16), vm((n_dp, hid_dev, quarter), BF16),
        vm((n_dp, quarter, hid_dev), BF16), vm((n_dp, quarter, hid_dev), BF16),
        vm((n_dp, voc_dev, quarter), F32), vm((n_dp, voc_dev, quarter), BF16), vm((n_dp, voc_dev, quarter), BF16),
        vm((n_dp, hid_dev, quarter), F32), vm((n_dp, quarter, hid_dev), F32),
        vm((n_dp, voc_dev, quarter), BF16), vm((n_dp, voc_dev, quarter), BF16),
        vm((n_dp, hid_dev, quarter), BF16), vm((n_dp, hid_dev, quarter), BF16),
        vm((n_dp, quarter, hid_dev), BF16), vm((n_dp, quarter, hid_dev), BF16),
        vm((8, rows), F32), vm((8, 128), F32), vm((8, 128), F32),
        pltpu.SemaphoreType.DMA((N_GROUPS, 2)), pltpu.SemaphoreType.DMA((N_GROUPS, 2)),
        pltpu.SemaphoreType.DMA((3,)), pltpu.SemaphoreType.DMA((3,)),
        pltpu.SemaphoreType.DMA((3,)), pltpu.SemaphoreType.DMA((3,)),
    ]
    return kernel, scratch


def solution(mesh):
    n_seg, n_mp, n_dp = mesh.shape["segment"], mesh.shape["mp"], mesh.shape["dp"]

    def on_device(text_rows, durations, unit_targets, w_in, w_out, w_unit):
        micro, rows, width = text_rows.shape
        units = unit_targets.shape[1]
        hid_dev = w_in.shape[2]
        voc_dev = w_unit.shape[1]
        denom = float(micro * units * n_dp)
        kernel, scratch = make_kernel(
            n_seg, n_mp // 2, n_dp, micro // 2, rows, width, hid_dev, voc_dev, units, denom
        )
        quarter = width // n_dp
        vmem = pl.BlockSpec(memory_space=pltpu.VMEM)
        loss, gin, gout, gun = pl.pallas_call(
            kernel,
            out_shape=(
                jax.ShapeDtypeStruct((8, 128), F32),
                jax.ShapeDtypeStruct((quarter, hid_dev), F32),
                jax.ShapeDtypeStruct((hid_dev, quarter), F32),
                jax.ShapeDtypeStruct((voc_dev, quarter), F32),
            ),
            in_specs=[pl.BlockSpec(memory_space=pl.ANY)] + [vmem] * 5,
            out_specs=(vmem,) * 4,
            scratch_shapes=scratch,
            compiler_params=pltpu.CompilerParams(
                collective_id=0, has_side_effects=True, vmem_limit_bytes=60 * 1024 * 1024
            ),
        )(
            text_rows, durations, unit_targets.reshape(micro, 1, units), w_in[0], w_out[0],
            jnp.transpose(w_unit),
        )
        return (loss[0, 0][None], gin[None], gout[None], jnp.transpose(gun))

    placed = (
        P(None, "dp", None),
        P(None, "dp", None),
        P(None, "dp"),
        P("segment", None, "mp"),
        P("segment", "mp", None),
        P(None, ("segment", "mp")),
    )
    return jax.shard_map(
        on_device,
        mesh=mesh,
        in_specs=placed,
        out_specs=(
            P("dp"),
            P("segment", "dp", "mp"),
            P("segment", "mp", "dp"),
            P("dp", ("segment", "mp")),
        ),
        check_vma=False,
    )
```

```python
import jax
import jax.numpy as jnp
from jax import lax
from jax.experimental import pallas as pl
from jax.experimental.pallas import tpu as pltpu
from jax.sharding import PartitionSpec as P

MESH = pl.DeviceIdType.MESH
F32 = jnp.float32
BF16 = jnp.bfloat16

(
    G_FRS, G_FAG, G_FINY, G_FINZ, G_STAT, G_NRS, G_NY, G_NAG, G_BRS, G_BAG, G_TEXT, G_LOSS, G_SIBW,
) = range(13)
N_GROUPS = 13


def gelu_parts(pre_vals):
    coeff = 0.7978845608
    inner = coeff * (pre_vals + 0.044715 * pre_vals * pre_vals * pre_vals)
    tanh_val = jnp.tanh(inner)
    value = 0.5 * pre_vals * (1.0 + tanh_val)
    slope = 0.5 * (1.0 + tanh_val) + 0.5 * pre_vals * (1.0 - tanh_val * tanh_val) * coeff * (
        1.0 + 3.0 * 0.044715 * pre_vals * pre_vals
    )
    return (value, slope)


def row_scale(floats):
    return lax.rsqrt(jnp.mean(floats * floats, axis=-1, keepdims=True) + 1e-06)


def norm_back(floats, grads):
    scale = row_scale(floats)
    normal = floats * scale
    return scale * (grads - normal * jnp.mean(grads * normal, axis=-1, keepdims=True))


def nn(a, b):
    return jnp.dot(a, b, preferred_element_type=F32)


def nt(a, b):
    return lax.dot_general(a, b, (((1,), (1,)), ((), ())), preferred_element_type=F32)


def tn(a, b):
    return lax.dot_general(a, b, (((0,), (0,)), ((), ())), preferred_element_type=F32)


def make_kernel(n_seg, n_z, n_dp, micros, chunks, rows, width, hid_dev, voc_dev, units, denom):
    all_rows = micros * rows
    cut = all_rows // chunks
    per = chunks // micros
    col = width // n_z
    n_peer = n_seg * n_z
    quarter = width // n_dp
    blocks = n_z // n_dp

    def kernel(
        text, dur, tgt, w_in, w_out, w_unit,
        loss_o, gin_o, gout_o, gun_o,
        wi_sib, wo_sib, wu_sib,
        xbuf, normed, part, rsf, osh, hid, slo,
        fin, fn, lg, cnt, stb, dlb, partd, rsd, ysend, yrecv, dxb, dsh,
        dpre, partb, rsb, bsh,
        gs_sib, gr_sib, gi_sib, gir_sib, gu_f, gu_sib, gur_sib, go_f, gi_f,
        xs_u, xr_u, xs_o, xr_o, xs_i, xr_i,
        lvec, lown, lrcv,
        ssem, rsem, sib_s, sib_r, dp_s, dp_r,
    ):
        s = lax.axis_index("segment")
        mp = lax.axis_index("mp")
        d = lax.axis_index("dp")
        z = lax.div(mp, 2)
        c = lax.rem(mp, 2)
        sib = 2 * z + (1 - c)
        me = s * n_z + z
        last = n_seg - 1

        def cds(k):
            return pl.ds(pl.multiple_of(k * cut, cut), cut)

        def mds(m):
            return pl.ds(pl.multiple_of(m * rows, rows), rows)

        def whole(buf, where):
            return jnp.concatenate([buf[i, where, :] for i in range(n_z)], axis=-1)

        def columns(i):
            return slice(i * col, (i + 1) * col)

        def put(src, dst, a, b, where):
            pltpu.make_async_remote_copy(
                src_ref=src, dst_ref=dst, send_sem=a, recv_sem=b, device_id=where, device_id_type=MESH
            ).start()

        def drain(ref, sem):
            pltpu.make_async_copy(ref, ref, sem).wait()

        def over(n, fn_of):
            def step(i, carry):
                fn_of(i)
                return carry

            lax.fori_loop(0, n, step, 0)

        def peers_z(fn_of):
            def step(i):
                side = 1 - 2 * lax.rem(i, 2)
                off = n_z // 2 + side * lax.div(i + 1, 2)
                fn_of(lax.rem(z + off, n_z))

            over(n_z - 1, step)

        barrier = pltpu.get_barrier_semaphore()

        def greet(where):
            pl.semaphore_signal(barrier, inc=1, device_id=where, device_id_type=MESH)

        peers_z(lambda z2: greet({"mp": 2 * z2 + c}))
        over(n_seg - 1, lambda i: greet({"segment": lax.rem(s + i + 1, n_seg)}))
        over(n_dp - 1, lambda i: greet({"dp": lax.rem(d + i + 1, n_dp)}))
        greet({"mp": sib})

        @pl.when(s == 0)
        def _():
            def load(k):
                for i in range(n_z):
                    pltpu.make_async_copy(
                        text.at[
                            micros * c + lax.div(k, per),
                            pl.ds(pl.multiple_of(lax.rem(k, per) * cut, cut), cut),
                            pl.ds(i * col, col),
                        ],
                        xbuf.at[i, cds(k)],
                        rsem.at[G_TEXT, k],
                    ).start()

            over(chunks, load)

        def count(k):
            lengths = dur[micros * c + k].astype(F32)
            lane = lax.broadcasted_iota(jnp.int32, (rows, rows), 1)
            sub = lax.broadcasted_iota(jnp.int32, (rows, rows), 0)
            tri = jnp.where(sub <= lane, 1.0, 0.0).astype(BF16)
            wide = jnp.broadcast_to(lengths, (8, rows)).astype(BF16)
            ends = nn(wide, tri)[0:1, :]
            starts = ends - lengths
            unit = lax.broadcasted_iota(jnp.int32, (units, rows), 0).astype(F32)
            onehot = jnp.where((starts <= unit) & (unit < ends), 1.0, 0.0).astype(BF16)
            target = tgt[pl.ds(micros * c + k, 1), :]
            ids = lax.broadcasted_iota(jnp.int32, (voc_dev, units), 0)
            for h, owner in ((0, mp), (1, sib)):
                first = (s * (2 * n_z) + owner) * voc_dev
                hits = jnp.where(ids + first == target, 1.0, 0.0).astype(BF16)
                cnt[k, h] = nn(hits, onehot)

        over(micros, count)
        pl.semaphore_wait(barrier, n_z - 1 + n_seg - 1 + n_dp - 1 + 1)

        put(w_in, wi_sib, ssem.at[G_SIBW, 0], rsem.at[G_SIBW, 0], {"mp": sib})
        put(w_out, wo_sib, ssem.at[G_SIBW, 1], rsem.at[G_SIBW, 1], {"mp": sib})
        put(w_unit, wu_sib, ssem.at[G_LOSS, 1], rsem.at[G_LOSS, 1], {"mp": sib})

        def scatter_z(buf, got, where, slot, group, k):
            own = got.at[slot, z]
            got[slot, z] = buf[z, where, :]
            peers_z(
                lambda z2: put(
                    buf.at[z2, where], own, ssem.at[group, k], rsem.at[group, k], {"mp": 2 * z2 + c}
                )
            )

        def owned_sum(buf, k):
            total = buf[k, 0].astype(F32)
            for i in range(1, n_z):
                total = total + buf[k, i].astype(F32)
            return total

        def forward(k):
            @pl.when(s == 0)
            def _():
                drain(xbuf.at[:, cds(k)], rsem.at[G_TEXT, k])

            @pl.when(s > 0)
            def _():
                drain(xbuf.at[:, cds(k)], rsem.at[G_FAG, k])

            x = whole(xbuf, cds(k)).astype(F32)
            n = (x * row_scale(x)).astype(BF16)
            normed[cds(k), :] = n

            value, slope = gelu_parts(nn(n, w_in[...]))
            h0 = value.astype(BF16)
            hid[0, cds(k), :] = h0
            slo[0, cds(k), :] = slope
            acc = nn(h0, w_out[...])

            @pl.when(k == 0)
            def _():
                drain(wi_sib, rsem.at[G_SIBW, 0])
                drain(wo_sib, rsem.at[G_SIBW, 1])

            value, slope = gelu_parts(nn(n, wi_sib[...]))
            h1 = value.astype(BF16)
            hid[1, cds(k), :] = h1
            slo[1, cds(k), :] = slope
            acc = (acc + nn(h1, wo_sib[...])).astype(BF16)
            for i in range(n_z):
                part[i, cds(k), :] = acc[:, columns(i)]
            scatter_z(part, rsf, cds(k), k, G_FRS, k)

        def forward_end(k):
            drain(rsf.at[k, pl.ds(0, n_z - 1)], rsem.at[G_FRS, k])
            x = xbuf[z, cds(k), :].astype(F32)
            new = (x + owned_sum(rsf, k)).astype(BF16)
            osh[k] = new

            @pl.when(s < last)
            def _():
                def send(z2):
                    put(
                        osh.at[k], xbuf.at[z, cds(k)], ssem.at[G_FAG, k], rsem.at[G_FAG, k],
                        {"segment": s + 1, "mp": 2 * z2 + c},
                    )

                peers_z(send)
                send(z)

            @pl.when(s == last)
            def _():
                fin[z, cds(k), :] = new

                def send(y2):
                    put(
                        osh.at[k], fin.at[z, cds(k)], ssem.at[G_FINY, k], rsem.at[G_FINY, k],
                        {"segment": y2},
                    )

                over(n_seg - 1, send)

        def staged(first, second):
            def step(i):
                @pl.when(i < chunks)
                def _():
                    first(i)

                @pl.when(i > 0)
                def _():
                    second(i - 1)

            over(chunks + 1, step)

        staged(forward, forward_end)
        drain(wu_sib, rsem.at[G_LOSS, 1])
        lvec[...] = jnp.zeros_like(lvec)

        def relay(k):
            @pl.when(s < last)
            def _():
                drain(fin.at[z, cds(k)], rsem.at[G_FINY, k])

            peers_z(
                lambda z2: put(
                    fin.at[z, cds(k)], fin.at[z, cds(k)], ssem.at[G_FINZ, k], rsem.at[G_FINZ, k],
                    {"mp": 2 * z2 + c},
                )
            )

        def logits(k):
            for j in range(per):
                drain(rsf.at[0, pl.ds(0, n_z - 1)], rsem.at[G_FINZ, k * per + j])
            x = whole(fin, mds(k)).astype(F32)
            n = (x * row_scale(x)).astype(BF16)
            fn[mds(k), :] = n
            a = nt(w_unit[...], n)
            b = nt(wu_sib[...], n)
            lg[k, 0] = a
            lg[k, 1] = b
            peak = jnp.maximum(jnp.max(a, axis=0, keepdims=True), jnp.max(b, axis=0, keepdims=True))
            total = jnp.sum(jnp.exp(a - peak), axis=0, keepdims=True) + jnp.sum(
                jnp.exp(b - peak), axis=0, keepdims=True
            )
            hit = jnp.sum(cnt[k, 0] * a, axis=0, keepdims=True) + jnp.sum(
                cnt[k, 1] * b, axis=0, keepdims=True
            )
            sub = lax.broadcasted_iota(jnp.int32, (8, rows), 0)
            stb[k, me] = jnp.where(sub == 0, peak, jnp.where(sub == 1, total, hit))

            def send(off):
                other = lax.rem(me + off + 1, n_peer)
                put(
                    stb.at[k, me], stb.at[k, me], ssem.at[G_STAT, k], rsem.at[G_STAT, k],
                    {"segment": lax.div(other, n_z), "mp": 2 * lax.rem(other, n_z) + c},
                )

            over(n_peer - 1, send)

        def dlogits(k):
            drain(stb.at[k, pl.ds(0, n_peer - 1)], rsem.at[G_STAT, k])
            every = stb[k]
            peaks = every[:, 0:1, :]
            peak = jnp.max(peaks, axis=0)
            total = jnp.sum(every[:, 1:2, :] * jnp.exp(peaks - peak[None]), axis=0)
            hit = jnp.sum(every[:, 2:3, :], axis=0)
            lse = peak + jnp.log(total)
            lengths = dur[micros * c + k].astype(F32)
            lvec[0:1, :] += lengths * lse - hit
            acc = None
            for h, w in ((0, w_unit), (1, wu_sib)):
                grad = (lengths * jnp.exp(lg[k, h] - lse) - cnt[k, h]) * (1.0 / denom)
                grad = grad.astype(BF16)
                dlb[h, k] = grad
                term = tn(grad, w[...])
                acc = term if acc is None else acc + term
            x = whole(fin, mds(k)).astype(F32)
            acc = norm_back(x, acc).astype(BF16)
            for i in range(n_z):
                partd[i, mds(k), :] = acc[:, columns(i)]
            scatter_z(partd, rsd, mds(k), k, G_NRS, k)

        def norm_sum(k):
            drain(rsd.at[k, pl.ds(0, n_z - 1)], rsem.at[G_NRS, k])
            ysend[k] = owned_sum(rsd, k).astype(BF16)

            @pl.when(s < last)
            def _():
                put(ysend.at[k], yrecv.at[k, s], ssem.at[G_NY, k], rsem.at[G_NY, k], {"segment": last})

        def norm_end(k):
            @pl.when(s == last)
            def _():
                drain(yrecv.at[k], rsem.at[G_NY, k])
                total = ysend[k].astype(F32)
                for i in range(n_seg - 1):
                    total = total + yrecv[k, i].astype(F32)
                grad = total.astype(BF16)
                dsh[k] = grad
                dxb[z, mds(k), :] = grad
                peers_z(
                    lambda z2: put(
                        dsh.at[k], dxb.at[z, mds(k)], ssem.at[G_NAG, k], rsem.at[G_NAG, k],
                        {"mp": 2 * z2 + c},
                    )
                )

        def dp_send(xs, xr, g):
            def step(off):
                d2 = lax.rem(d + off + 1, n_dp)
                put(xs.at[d2], xr.at[d], dp_s.at[g], dp_r.at[g], {"dp": d2})

            over(n_dp - 1, step)

        def dp_out(own, xr, g, out):
            drain(xr.at[pl.ds(0, n_dp - 1)], dp_r.at[g])
            total = own
            for off in range(1, n_dp):
                total = total + xr[lax.rem(d + off, n_dp)].astype(F32)
            out[...] = total

        def unit_grad():
            lown[...] = jnp.broadcast_to(jnp.sum(lvec[...], keepdims=True), lown.shape)
            put(lown, lrcv, ssem.at[G_LOSS, 0], rsem.at[G_LOSS, 0], {"mp": sib})
            for h in (1, 0):
                total = nn(dlb[h, 0], fn[pl.ds(0, rows), :])
                for k in range(1, micros):
                    total = total + nn(dlb[h, k], fn[pl.ds(k * rows, rows), :])
                for q in range(n_dp):
                    piece = total[:, q * quarter : (q + 1) * quarter]
                    if h == 1:
                        gu_sib[q] = piece.astype(BF16)
                    else:
                        gu_f[q] = piece
                if h == 1:
                    put(gu_sib, gur_sib, sib_s.at[0], sib_r.at[0], {"mp": sib})
            drain(gur_sib, sib_r.at[0])

            def unit_sum(q):
                total = gu_f[q] + gur_sib[q].astype(F32)
                gu_f[q] = total
                xs_u[q] = total.astype(BF16)

            over(n_dp, unit_sum)
            dp_send(xs_u, xr_u, 0)

        for k in range(per + 1):
            relay(k)
        logits(0)
        for k in range(per + 1, chunks):
            relay(k)
        dlogits(0)
        logits(1)
        norm_sum(0)
        dlogits(1)
        norm_end(0)
        norm_sum(1)
        norm_end(1)

        @pl.when(s < last)
        def _():
            unit_grad()

        def backward(k):
            @pl.when((s == last) & (lax.rem(k, per) == 0))
            def _():
                drain(rsd.at[0, pl.ds(0, n_z - 1)], rsem.at[G_NAG, lax.div(k, per)])

            @pl.when(s < last)
            def _():
                drain(dxb.at[:, cds(k)], rsem.at[G_BAG, k])

            g = whole(dxb, cds(k))
            p0 = (nt(g, w_out[...]) * slo[0, cds(k), :]).astype(BF16)
            dpre[0, cds(k), :] = p0
            p1 = (nt(g, wo_sib[...]) * slo[1, cds(k), :]).astype(BF16)
            dpre[1, cds(k), :] = p1

            @pl.when(s > 0)
            def _():
                x = whole(xbuf, cds(k)).astype(F32)
                acc = norm_back(x, nt(p0, w_in[...]) + nt(p1, wi_sib[...])).astype(BF16)
                for i in range(n_z):
                    partb[i, cds(k), :] = acc[:, columns(i)]
                scatter_z(partb, rsb, cds(k), k, G_BRS, k)

        def backward_end(k):
            @pl.when(s > 0)
            def _():
                drain(rsb.at[k, pl.ds(0, n_z - 1)], rsem.at[G_BRS, k])
                bsh[k] = (dxb[z, cds(k), :].astype(F32) + owned_sum(rsb, k)).astype(BF16)

                def send(z2):
                    put(
                        bsh.at[k], dxb.at[z, cds(k)], ssem.at[G_BAG, k], rsem.at[G_BAG, k],
                        {"segment": s - 1, "mp": 2 * z2 + c},
                    )

                peers_z(send)
                send(z)

        staged(backward, backward_end)

        @pl.when(s == last)
        def _():
            unit_grad()

        def grad_columns(q):
            return jnp.concatenate([dxb[q * blocks + i] for i in range(blocks)], axis=-1)

        for q in range(n_dp):
            gs_sib[q] = tn(hid[1], grad_columns(q)).astype(BF16)
        put(gs_sib, gr_sib, sib_s.at[1], sib_r.at[1], {"mp": sib})
        for q in range(n_dp):
            go_f[q] = tn(hid[0], grad_columns(q))
        for q in range(n_dp):
            gi_sib[q] = tn(normed[:, q * quarter : (q + 1) * quarter], dpre[1]).astype(BF16)
        put(gi_sib, gir_sib, sib_s.at[2], sib_r.at[2], {"mp": sib})
        drain(gr_sib, sib_r.at[1])

        def out_sum(q):
            total = go_f[q] + gr_sib[q].astype(F32)
            go_f[q] = total
            xs_o[q] = total.astype(BF16)

        over(n_dp, out_sum)
        dp_send(xs_o, xr_o, 1)
        for q in range(n_dp):
            gi_f[q] = tn(normed[:, q * quarter : (q + 1) * quarter], dpre[0])
        drain(gir_sib, sib_r.at[2])

        def in_sum(q):
            total = gi_f[q] + gir_sib[q].astype(F32)
            gi_f[q] = total
            xs_i[q] = total.astype(BF16)

        over(n_dp, in_sum)
        dp_send(xs_i, xr_i, 2)

        dp_out(gu_f[d], xr_u, 0, gun_o)
        drain(lrcv, rsem.at[G_LOSS, 0])
        loss_o[0] = jnp.max(lown[...] + lrcv[...]) * (1.0 / denom)
        dp_out(go_f[d], xr_o, 1, gout_o)
        dp_out(gi_f[d], xr_i, 2, gin_o)

        drain(w_in, ssem.at[G_SIBW, 0])
        drain(w_out, ssem.at[G_SIBW, 1])
        drain(w_unit, ssem.at[G_LOSS, 1])
        drain(lown, ssem.at[G_LOSS, 0])
        drain(gu_sib, sib_s.at[0])
        drain(gs_sib, sib_s.at[1])
        drain(gi_sib, sib_s.at[2])
        drain(xs_u.at[pl.ds(0, n_dp - 1)], dp_s.at[0])
        drain(xs_o.at[pl.ds(0, n_dp - 1)], dp_s.at[1])
        drain(xs_i.at[pl.ds(0, n_dp - 1)], dp_s.at[2])

        def finish(k):
            part_of = rsf.at[0, pl.ds(0, n_z - 1)]
            drain(part_of, ssem.at[G_FRS, k])
            drain(part_of, ssem.at[G_FINZ, k])

            @pl.when(s < last)
            def _():
                drain(rsf.at[0], ssem.at[G_FAG, k])

            @pl.when(s == last)
            def _():
                drain(osh.at[pl.ds(0, n_seg - 1)], ssem.at[G_FINY, k])

            @pl.when(s > 0)
            def _():
                drain(part_of, ssem.at[G_BRS, k])
                drain(rsf.at[0], ssem.at[G_BAG, k])

        def finish_micro(k):
            part_of = rsd.at[0, pl.ds(0, n_z - 1)]
            drain(part_of, ssem.at[G_NRS, k])
            drain(stb.at[k, pl.ds(0, n_peer - 1)], ssem.at[G_STAT, k])

            @pl.when(s < last)
            def _():
                drain(ysend.at[k], ssem.at[G_NY, k])

            @pl.when(s == last)
            def _():
                drain(part_of, ssem.at[G_NAG, k])

        over(chunks, finish)
        over(micros, finish_micro)

    vm = pltpu.VMEM
    lines = (n_z, all_rows, col)
    shard = (chunks, cut, col)
    mshard = (micros, rows, col)
    scatter = (chunks, n_z, cut, col)
    mscatter = (micros, n_z, rows, col)
    scratch = [
        vm((width, hid_dev), BF16), vm((hid_dev, width), BF16), vm((voc_dev, width), BF16),
        vm(lines, BF16), vm((all_rows, width), BF16), vm(lines, BF16),
        vm(scatter, BF16), vm(shard, BF16), vm((2, all_rows, hid_dev), BF16), vm((2, all_rows, hid_dev), F32),
        vm(lines, BF16), vm((all_rows, width), BF16),
        vm((micros, 2, voc_dev, rows), F32), vm((micros, 2, voc_dev, rows), F32),
        vm((micros, n_peer, 8, rows), F32), vm((2, micros, voc_dev, rows), BF16),
        vm(lines, BF16), vm(mscatter, BF16), vm(mshard, BF16),
        vm((micros, n_seg - 1, rows, col), BF16), vm(lines, BF16), vm(mshard, BF16),
        vm((2, all_rows, hid_dev), BF16), vm(lines, BF16), vm(scatter, BF16), vm(shard, BF16),
        vm((n_dp, hid_dev, quarter), BF16), vm((n_dp, hid_dev, quarter), BF16),
        vm((n_dp, quarter, hid_dev), BF16), vm((n_dp, quarter, hid_dev), BF16),
        vm((n_dp, voc_dev, quarter), F32), vm((n_dp, voc_dev, quarter), BF16), vm((n_dp, voc_dev, quarter), BF16),
        vm((n_dp, hid_dev, quarter), F32), vm((n_dp, quarter, hid_dev), F32),
        vm((n_dp, voc_dev, quarter), BF16), vm((n_dp, voc_dev, quarter), BF16),
        vm((n_dp, hid_dev, quarter), BF16), vm((n_dp, hid_dev, quarter), BF16),
        vm((n_dp, quarter, hid_dev), BF16), vm((n_dp, quarter, hid_dev), BF16),
        vm((8, rows), F32), vm((8, 128), F32), vm((8, 128), F32),
        pltpu.SemaphoreType.DMA((N_GROUPS, chunks)), pltpu.SemaphoreType.DMA((N_GROUPS, chunks)),
        pltpu.SemaphoreType.DMA((3,)), pltpu.SemaphoreType.DMA((3,)),
        pltpu.SemaphoreType.DMA((3,)), pltpu.SemaphoreType.DMA((3,)),
    ]
    return kernel, scratch


def solution(mesh):
    n_seg, n_mp, n_dp = mesh.shape["segment"], mesh.shape["mp"], mesh.shape["dp"]

    def on_device(text_rows, durations, unit_targets, w_in, w_out, w_unit):
        micro, rows, width = text_rows.shape
        units = unit_targets.shape[1]
        hid_dev = w_in.shape[2]
        voc_dev = w_unit.shape[1]
        denom = float(micro * units * n_dp)
        kernel, scratch = make_kernel(
            n_seg, n_mp // 2, n_dp, micro // 2, 4, rows, width, hid_dev, voc_dev, units, denom
        )
        quarter = width // n_dp
        vmem = pl.BlockSpec(memory_space=pltpu.VMEM)
        loss, gin, gout, gun = pl.pallas_call(
            kernel,
            out_shape=(
                jax.ShapeDtypeStruct((1,), F32),
                jax.ShapeDtypeStruct((quarter, hid_dev), F32),
                jax.ShapeDtypeStruct((hid_dev, quarter), F32),
                jax.ShapeDtypeStruct((voc_dev, quarter), F32),
            ),
            in_specs=[pl.BlockSpec(memory_space=pl.ANY)] + [vmem] * 5,
            out_specs=(pl.BlockSpec(memory_space=pltpu.SMEM), vmem, vmem, vmem),
            scratch_shapes=scratch,
            compiler_params=pltpu.CompilerParams(
                collective_id=0, has_side_effects=True, vmem_limit_bytes=60 * 1024 * 1024
            ),
        )(
            text_rows, durations, unit_targets, w_in[0], w_out[0],
            jnp.transpose(w_unit),
        )
        return (loss, gin[None], gout[None], jnp.transpose(gun))

    placed = (
        P(None, "dp", None),
        P(None, "dp", None),
        P(None, "dp"),
        P("segment", None, "mp"),
        P("segment", "mp", None),
        P(None, ("segment", "mp")),
    )
    return jax.shard_map(
        on_device,
        mesh=mesh,
        in_specs=placed,
        out_specs=(
            P("dp"),
            P("segment", "dp", "mp"),
            P("segment", "mp", "dp"),
            P("dp", ("segment", "mp")),
        ),
        check_vma=False,
    )
```

```python
import jax
import jax.numpy as jnp
from jax import lax
from jax.experimental import pallas as pl
from jax.experimental.pallas import tpu as pltpu
from jax.sharding import PartitionSpec as P

MESH = pl.DeviceIdType.MESH
F32 = jnp.float32
BF16 = jnp.bfloat16

(
    G_FRS, G_FAG, G_FINY, G_FINZ, G_STAT, G_NRS, G_NY, G_NAG, G_BRS, G_BAG, G_TEXT, G_LOSS, G_SIBW,
) = range(13)
N_GROUPS = 13


def gelu_parts(pre_vals):
    coeff = 0.7978845608
    inner = coeff * (pre_vals + 0.044715 * pre_vals * pre_vals * pre_vals)
    tanh_val = jnp.tanh(inner)
    value = 0.5 * pre_vals * (1.0 + tanh_val)
    slope = 0.5 * (1.0 + tanh_val) + 0.5 * pre_vals * (1.0 - tanh_val * tanh_val) * coeff * (
        1.0 + 3.0 * 0.044715 * pre_vals * pre_vals
    )
    return (value, slope)


def row_scale(floats):
    return lax.rsqrt(jnp.mean(floats * floats, axis=-1, keepdims=True) + 1e-06)


def norm_back(floats, grads):
    scale = row_scale(floats)
    normal = floats * scale
    return scale * (grads - normal * jnp.mean(grads * normal, axis=-1, keepdims=True))


def nn(a, b):
    return jnp.dot(a, b, preferred_element_type=F32)


def nt(a, b):
    return lax.dot_general(a, b, (((1,), (1,)), ((), ())), preferred_element_type=F32)


def tn(a, b):
    return lax.dot_general(a, b, (((0,), (0,)), ((), ())), preferred_element_type=F32)


def make_kernel(n_seg, n_z, n_dp, micros, chunks, rows, width, hid_dev, voc_dev, units, denom):
    all_rows = micros * rows
    cut = all_rows // chunks
    per = chunks // micros
    col = width // n_z
    n_peer = n_seg * n_z
    quarter = width // n_dp
    blocks = n_z // n_dp

    def kernel(
        text, dur, tgt, w_in, w_out, w_unit,
        loss_o, gin_o, gout_o, gun_o,
        wi_sib, wo_sib, wu_sib,
        xbuf, normed, part, rsf, osh, hid, slo,
        fin, fn, lg, cnt, stb, dlb, partd, rsd, ysend, yrecv, dxb, dsh,
        dpre, partb, rsb, bsh,
        gs_sib, gr_sib, gi_sib, gir_sib, gu_f, gu_sib, gur_sib, go_f, gi_f,
        xs_u, xr_u, xs_o, xr_o, xs_i, xr_i,
        lvec, lown, lrcv,
        ssem, rsem, sib_s, sib_r, dp_s, dp_r,
    ):
        s = lax.axis_index("segment")
        mp = lax.axis_index("mp")
        d = lax.axis_index("dp")
        z = lax.div(mp, 2)
        c = lax.rem(mp, 2)
        sib = 2 * z + (1 - c)
        me = s * n_z + z
        last = n_seg - 1

        def cds(k):
            return pl.ds(pl.multiple_of(k * cut, cut), cut)

        def mds(m):
            return pl.ds(pl.multiple_of(m * rows, rows), rows)

        def whole(buf, where):
            return jnp.concatenate([buf[i, where, :] for i in range(n_z)], axis=-1)

        def columns(i):
            return slice(i * col, (i + 1) * col)

        def put(src, dst, a, b, where):
            pltpu.make_async_remote_copy(
                src_ref=src, dst_ref=dst, send_sem=a, recv_sem=b, device_id=where, device_id_type=MESH
            ).start()

        def drain(ref, sem):
            pltpu.make_async_copy(ref, ref, sem).wait()

        def span(start, stop, fn_of):
            def step(i, carry):
                fn_of(i)
                return carry

            lax.fori_loop(start, stop, step, 0)

        def over(n, fn_of):
            span(0, n, fn_of)

        def peers_z(fn_of):
            def step(i):
                side = 1 - 2 * lax.rem(i, 2)
                off = n_z // 2 + side * lax.div(i + 1, 2)
                fn_of(lax.rem(z + off, n_z))

            over(n_z - 1, step)

        barrier = pltpu.get_barrier_semaphore()

        def greet(where):
            pl.semaphore_signal(barrier, inc=1, device_id=where, device_id_type=MESH)

        peers_z(lambda z2: greet({"mp": 2 * z2 + c}))
        over(n_seg - 1, lambda i: greet({"segment": lax.rem(s + i + 1, n_seg)}))
        over(n_dp - 1, lambda i: greet({"dp": lax.rem(d + i + 1, n_dp)}))
        greet({"mp": sib})

        @pl.when(s == 0)
        def _():
            def load(k):
                for i in range(n_z):
                    pltpu.make_async_copy(
                        text.at[
                            micros * c + lax.div(k, per),
                            pl.ds(pl.multiple_of(lax.rem(k, per) * cut, cut), cut),
                            pl.ds(i * col, col),
                        ],
                        xbuf.at[i, cds(k)],
                        rsem.at[G_TEXT, k],
                    ).start()

            over(chunks, load)

        def count(k):
            lengths = dur[micros * c + k].astype(F32)
            lane = lax.broadcasted_iota(jnp.int32, (rows, rows), 1)
            sub = lax.broadcasted_iota(jnp.int32, (rows, rows), 0)
            tri = jnp.where(sub <= lane, 1.0, 0.0).astype(BF16)
            wide = jnp.broadcast_to(lengths, (8, rows)).astype(BF16)
            ends = nn(wide, tri)[0:1, :]
            starts = ends - lengths
            unit = lax.broadcasted_iota(jnp.int32, (units, rows), 0).astype(F32)
            onehot = jnp.where((starts <= unit) & (unit < ends), 1.0, 0.0).astype(BF16)
            target = tgt[pl.ds(micros * c + k, 1), :]
            ids = lax.broadcasted_iota(jnp.int32, (voc_dev, units), 0)
            for h, owner in ((0, mp), (1, sib)):
                first = (s * (2 * n_z) + owner) * voc_dev
                hits = jnp.where(ids + first == target, 1.0, 0.0).astype(BF16)
                cnt[k, h] = nn(hits, onehot)

        over(micros, count)
        pl.semaphore_wait(barrier, n_z - 1 + n_seg - 1 + n_dp - 1 + 1)

        put(w_in, wi_sib, ssem.at[G_SIBW, 0], rsem.at[G_SIBW, 0], {"mp": sib})
        put(w_out, wo_sib, ssem.at[G_SIBW, 1], rsem.at[G_SIBW, 1], {"mp": sib})
        put(w_unit, wu_sib, ssem.at[G_LOSS, 1], rsem.at[G_LOSS, 1], {"mp": sib})

        def scatter_z(buf, got, where, slot, group, k):
            own = got.at[slot, z]
            got[slot, z] = buf[z, where, :]
            peers_z(
                lambda z2: put(
                    buf.at[z2, where], own, ssem.at[group, k], rsem.at[group, k], {"mp": 2 * z2 + c}
                )
            )

        def in_plane(src, dst, group, k):
            peers_z(
                lambda z2: put(src, dst, ssem.at[group, k], rsem.at[group, k], {"mp": 2 * z2 + c})
            )

        def owned_sum(buf, k):
            total = buf[k, 0].astype(F32)
            for i in range(1, n_z):
                total = total + buf[k, i].astype(F32)
            return total

        def forward(k):
            @pl.when(s == 0)
            def _():
                drain(xbuf.at[:, cds(k)], rsem.at[G_TEXT, k])

            @pl.when(s > 0)
            def _():
                drain(xbuf.at[:, cds(k)], rsem.at[G_FAG, k])

            x = whole(xbuf, cds(k)).astype(F32)
            n = (x * row_scale(x)).astype(BF16)
            normed[cds(k), :] = n

            value, slope = gelu_parts(nn(n, w_in[...]))
            h0 = value.astype(BF16)
            hid[0, cds(k), :] = h0
            slo[0, cds(k), :] = slope
            acc = nn(h0, w_out[...])

            @pl.when(k == 0)
            def _():
                drain(wi_sib, rsem.at[G_SIBW, 0])
                drain(wo_sib, rsem.at[G_SIBW, 1])

            value, slope = gelu_parts(nn(n, wi_sib[...]))
            h1 = value.astype(BF16)
            hid[1, cds(k), :] = h1
            slo[1, cds(k), :] = slope
            acc = (acc + nn(h1, wo_sib[...])).astype(BF16)
            for i in range(n_z):
                part[i, cds(k), :] = acc[:, columns(i)]
            scatter_z(part, rsf, cds(k), k, G_FRS, k)

        def forward_end(k):
            drain(rsf.at[k, pl.ds(0, n_z - 1)], rsem.at[G_FRS, k])
            x = xbuf[z, cds(k), :].astype(F32)
            new = (x + owned_sum(rsf, k)).astype(BF16)
            osh[k] = new

            @pl.when(s < last)
            def _():
                def send(z2):
                    put(
                        osh.at[k], xbuf.at[z, cds(k)], ssem.at[G_FAG, k], rsem.at[G_FAG, k],
                        {"segment": s + 1, "mp": 2 * z2 + c},
                    )

                peers_z(send)
                send(z)

            @pl.when(s == last)
            def _():
                fin[z, cds(k), :] = new

                def send(y2):
                    put(
                        osh.at[k], fin.at[z, cds(k)], ssem.at[G_FINY, k], rsem.at[G_FINY, k],
                        {"segment": y2},
                    )

                over(n_seg - 1, send)
                in_plane(osh.at[k], fin.at[z, cds(k)], G_FINZ, k)

        def staged(first, second, start, stop):
            def step(i):
                @pl.when(i < chunks)
                def _():
                    first(i)

                @pl.when(i > 0)
                def _():
                    second(i - 1)

            span(start, stop, step)


        def relay(k):
            drain(fin.at[z, cds(k)], rsem.at[G_FINY, k])
            in_plane(fin.at[z, cds(k)], fin.at[z, cds(k)], G_FINZ, k)

        def logits(k):
            for j in range(per):
                drain(rsf.at[0, pl.ds(0, n_z - 1)], rsem.at[G_FINZ, k * per + j])
            x = whole(fin, mds(k)).astype(F32)
            n = (x * row_scale(x)).astype(BF16)
            fn[mds(k), :] = n
            a = nt(w_unit[...], n)
            b = nt(wu_sib[...], n)
            lg[k, 0] = a
            lg[k, 1] = b
            peak = jnp.maximum(jnp.max(a, axis=0, keepdims=True), jnp.max(b, axis=0, keepdims=True))
            total = jnp.sum(jnp.exp(a - peak), axis=0, keepdims=True) + jnp.sum(
                jnp.exp(b - peak), axis=0, keepdims=True
            )
            hit = jnp.sum(cnt[k, 0] * a, axis=0, keepdims=True) + jnp.sum(
                cnt[k, 1] * b, axis=0, keepdims=True
            )
            sub = lax.broadcasted_iota(jnp.int32, (8, rows), 0)
            stb[k, me] = jnp.where(sub == 0, peak, jnp.where(sub == 1, total, hit))

            def send(off):
                other = lax.rem(me + off + 1, n_peer)
                put(
                    stb.at[k, me], stb.at[k, me], ssem.at[G_STAT, k], rsem.at[G_STAT, k],
                    {"segment": lax.div(other, n_z), "mp": 2 * lax.rem(other, n_z) + c},
                )

            over(n_peer - 1, send)

        def dlogits(k):
            drain(stb.at[k, pl.ds(0, n_peer - 1)], rsem.at[G_STAT, k])
            every = stb[k]
            peaks = every[:, 0:1, :]
            peak = jnp.max(peaks, axis=0)
            total = jnp.sum(every[:, 1:2, :] * jnp.exp(peaks - peak[None]), axis=0)
            hit = jnp.sum(every[:, 2:3, :], axis=0)
            lse = peak + jnp.log(total)
            lengths = dur[micros * c + k].astype(F32)
            lvec[0:1, :] += lengths * lse - hit
            acc = None
            for h, w in ((0, w_unit), (1, wu_sib)):
                grad = (lengths * jnp.exp(lg[k, h] - lse) - cnt[k, h]) * (1.0 / denom)
                grad = grad.astype(BF16)
                dlb[h, k] = grad
                term = tn(grad, w[...])
                acc = term if acc is None else acc + term
            x = whole(fin, mds(k)).astype(F32)
            acc = norm_back(x, acc).astype(BF16)
            for i in range(n_z):
                partd[i, mds(k), :] = acc[:, columns(i)]
            span(k * per, (k + 1) * per, lambda j: scatter_z(partd, rsd, cds(j), j, G_NRS, j))

        def norm_sum(k):
            drain(rsd.at[k, pl.ds(0, n_z - 1)], rsem.at[G_NRS, k])
            ysend[k] = owned_sum(rsd, k).astype(BF16)

            @pl.when(s < last)
            def _():
                put(ysend.at[k], yrecv.at[k, s], ssem.at[G_NY, k], rsem.at[G_NY, k], {"segment": last})

        def norm_end(k):
            drain(yrecv.at[k], rsem.at[G_NY, k])
            total = ysend[k].astype(F32)
            for i in range(n_seg - 1):
                total = total + yrecv[k, i].astype(F32)
            grad = total.astype(BF16)
            dsh[k] = grad
            dxb[z, cds(k), :] = grad
            in_plane(dsh.at[k], dxb.at[z, cds(k)], G_NAG, k)

        def dp_send(xs, xr, g):
            def step(off):
                d2 = lax.rem(d + off + 1, n_dp)
                put(xs.at[d2], xr.at[d], dp_s.at[g], dp_r.at[g], {"dp": d2})

            over(n_dp - 1, step)

        def dp_out(own, xr, g, out):
            drain(xr.at[pl.ds(0, n_dp - 1)], dp_r.at[g])
            total = own
            for off in range(1, n_dp):
                total = total + xr[lax.rem(d + off, n_dp)].astype(F32)
            out[...] = total

        def unit_grad():
            lown[...] = jnp.broadcast_to(jnp.sum(lvec[...], keepdims=True), lown.shape)
            put(lown, lrcv, ssem.at[G_LOSS, 0], rsem.at[G_LOSS, 0], {"mp": sib})
            for h in (1, 0):
                total = nn(dlb[h, 0], fn[pl.ds(0, rows), :])
                for k in range(1, micros):
                    total = total + nn(dlb[h, k], fn[pl.ds(k * rows, rows), :])
                for q in range(n_dp):
                    piece = total[:, q * quarter : (q + 1) * quarter]
                    if h == 1:
                        gu_sib[q] = piece.astype(BF16)
                    else:
                        gu_f[q] = piece
                if h == 1:
                    put(gu_sib, gur_sib, sib_s.at[0], sib_r.at[0], {"mp": sib})
            drain(gur_sib, sib_r.at[0])

            def unit_sum(q):
                total = gu_f[q] + gur_sib[q].astype(F32)
                gu_f[q] = total
                xs_u[q] = total.astype(BF16)

            over(n_dp, unit_sum)
            dp_send(xs_u, xr_u, 0)

        def backward(k):
            @pl.when(s == last)
            def _():
                drain(rsd.at[0, pl.ds(0, n_z - 1)], rsem.at[G_NAG, k])

            @pl.when(s < last)
            def _():
                drain(dxb.at[:, cds(k)], rsem.at[G_BAG, k])

            g = whole(dxb, cds(k))
            p0 = (nt(g, w_out[...]) * slo[0, cds(k), :]).astype(BF16)
            dpre[0, cds(k), :] = p0
            p1 = (nt(g, wo_sib[...]) * slo[1, cds(k), :]).astype(BF16)
            dpre[1, cds(k), :] = p1

            @pl.when(s > 0)
            def _():
                x = whole(xbuf, cds(k)).astype(F32)
                acc = norm_back(x, nt(p0, w_in[...]) + nt(p1, wi_sib[...])).astype(BF16)
                for i in range(n_z):
                    partb[i, cds(k), :] = acc[:, columns(i)]
                scatter_z(partb, rsb, cds(k), k, G_BRS, k)

        def backward_end(k):
            @pl.when(s > 0)
            def _():
                drain(rsb.at[k, pl.ds(0, n_z - 1)], rsem.at[G_BRS, k])
                bsh[k] = (dxb[z, cds(k), :].astype(F32) + owned_sum(rsb, k)).astype(BF16)

                def send(z2):
                    put(
                        bsh.at[k], dxb.at[z, cds(k)], ssem.at[G_BAG, k], rsem.at[G_BAG, k],
                        {"segment": s - 1, "mp": 2 * z2 + c},
                    )

                peers_z(send)
                send(z)

        early = per + per // 2
        staged(forward, forward_end, 0, early + 1)
        drain(wu_sib, rsem.at[G_LOSS, 1])
        lvec[...] = jnp.zeros_like(lvec)

        @pl.when(s == last)
        def _():
            logits(0)

        staged(forward, forward_end, early + 1, chunks + 1)

        @pl.when(s < last)
        def _():
            over(early, relay)
            logits(0)
            span(early, chunks, relay)

        dlogits(0)
        logits(1)

        @pl.when(s < last)
        def _():
            over(per - 1, norm_sum)
            dlogits(1)
            span(per - 1, chunks, norm_sum)
            unit_grad()
            staged(backward, backward_end, 0, chunks + 1)

        @pl.when(s == last)
        def _():
            over(per - 1, norm_sum)
            norm_end(0)
            dlogits(1)
            norm_sum(per - 1)
            span(1, per, norm_end)

            def first_half(i):
                backward(i)
                norm_sum(per + i)

            over(per, first_half)

            def second_half(i):
                norm_end(per + i)
                backward_end(i)

            over(per, second_half)
            span(per, chunks, backward)
            span(per, chunks, backward_end)
            unit_grad()

        def grad_columns(q):
            return jnp.concatenate([dxb[q * blocks + i] for i in range(blocks)], axis=-1)

        for q in range(n_dp):
            gs_sib[q] = tn(hid[1], grad_columns(q)).astype(BF16)
        put(gs_sib, gr_sib, sib_s.at[1], sib_r.at[1], {"mp": sib})
        for q in range(n_dp):
            go_f[q] = tn(hid[0], grad_columns(q))
        for q in range(n_dp):
            gi_sib[q] = tn(normed[:, q * quarter : (q + 1) * quarter], dpre[1]).astype(BF16)
        put(gi_sib, gir_sib, sib_s.at[2], sib_r.at[2], {"mp": sib})
        drain(gr_sib, sib_r.at[1])

        def out_sum(q):
            total = go_f[q] + gr_sib[q].astype(F32)
            go_f[q] = total
            xs_o[q] = total.astype(BF16)

        over(n_dp, out_sum)
        dp_send(xs_o, xr_o, 1)
        for q in range(n_dp):
            gi_f[q] = tn(normed[:, q * quarter : (q + 1) * quarter], dpre[0])
        drain(gir_sib, sib_r.at[2])

        def in_sum(q):
            total = gi_f[q] + gir_sib[q].astype(F32)
            gi_f[q] = total
            xs_i[q] = total.astype(BF16)

        over(n_dp, in_sum)
        dp_send(xs_i, xr_i, 2)

        dp_out(gu_f[d], xr_u, 0, gun_o)
        drain(lrcv, rsem.at[G_LOSS, 0])
        loss_o[0] = jnp.max(lown[...] + lrcv[...]) * (1.0 / denom)
        dp_out(go_f[d], xr_o, 1, gout_o)
        dp_out(gi_f[d], xr_i, 2, gin_o)

        drain(w_in, ssem.at[G_SIBW, 0])
        drain(w_out, ssem.at[G_SIBW, 1])
        drain(w_unit, ssem.at[G_LOSS, 1])
        drain(lown, ssem.at[G_LOSS, 0])
        drain(gu_sib, sib_s.at[0])
        drain(gs_sib, sib_s.at[1])
        drain(gi_sib, sib_s.at[2])
        drain(xs_u.at[pl.ds(0, n_dp - 1)], dp_s.at[0])
        drain(xs_o.at[pl.ds(0, n_dp - 1)], dp_s.at[1])
        drain(xs_i.at[pl.ds(0, n_dp - 1)], dp_s.at[2])

        def finish(k):
            part_of = rsf.at[0, pl.ds(0, n_z - 1)]
            drain(part_of, ssem.at[G_FRS, k])
            drain(part_of, ssem.at[G_FINZ, k])

            drain(part_of, ssem.at[G_NRS, k])

            @pl.when(s < last)
            def _():
                drain(rsf.at[0], ssem.at[G_FAG, k])
                drain(ysend.at[k], ssem.at[G_NY, k])

            @pl.when(s == last)
            def _():
                drain(osh.at[pl.ds(0, n_seg - 1)], ssem.at[G_FINY, k])
                drain(part_of, ssem.at[G_NAG, k])

            @pl.when(s > 0)
            def _():
                drain(part_of, ssem.at[G_BRS, k])
                drain(rsf.at[0], ssem.at[G_BAG, k])

        def finish_micro(k):
            drain(stb.at[k, pl.ds(0, n_peer - 1)], ssem.at[G_STAT, k])

        over(chunks, finish)
        over(micros, finish_micro)

    vm = pltpu.VMEM
    lines = (n_z, all_rows, col)
    shard = (chunks, cut, col)
    scatter = (chunks, n_z, cut, col)
    scratch = [
        vm((width, hid_dev), BF16), vm((hid_dev, width), BF16), vm((voc_dev, width), BF16),
        vm(lines, BF16), vm((all_rows, width), BF16), vm(lines, BF16),
        vm(scatter, BF16), vm(shard, BF16), vm((2, all_rows, hid_dev), BF16), vm((2, all_rows, hid_dev), F32),
        vm(lines, BF16), vm((all_rows, width), BF16),
        vm((micros, 2, voc_dev, rows), F32), vm((micros, 2, voc_dev, rows), F32),
        vm((micros, n_peer, 8, rows), F32), vm((2, micros, voc_dev, rows), BF16),
        vm(lines, BF16), vm(scatter, BF16), vm(shard, BF16),
        vm((chunks, n_seg - 1, cut, col), BF16), vm(lines, BF16), vm(shard, BF16),
        vm((2, all_rows, hid_dev), BF16), vm(lines, BF16), vm(scatter, BF16), vm(shard, BF16),
        vm((n_dp, hid_dev, quarter), BF16), vm((n_dp, hid_dev, quarter), BF16),
        vm((n_dp, quarter, hid_dev), BF16), vm((n_dp, quarter, hid_dev), BF16),
        vm((n_dp, voc_dev, quarter), F32), vm((n_dp, voc_dev, quarter), BF16), vm((n_dp, voc_dev, quarter), BF16),
        vm((n_dp, hid_dev, quarter), F32), vm((n_dp, quarter, hid_dev), F32),
        vm((n_dp, voc_dev, quarter), BF16), vm((n_dp, voc_dev, quarter), BF16),
        vm((n_dp, hid_dev, quarter), BF16), vm((n_dp, hid_dev, quarter), BF16),
        vm((n_dp, quarter, hid_dev), BF16), vm((n_dp, quarter, hid_dev), BF16),
        vm((8, rows), F32), vm((8, 128), F32), vm((8, 128), F32),
        pltpu.SemaphoreType.DMA((N_GROUPS, chunks)), pltpu.SemaphoreType.DMA((N_GROUPS, chunks)),
        pltpu.SemaphoreType.DMA((3,)), pltpu.SemaphoreType.DMA((3,)),
        pltpu.SemaphoreType.DMA((3,)), pltpu.SemaphoreType.DMA((3,)),
    ]
    return kernel, scratch


def solution(mesh):
    n_seg, n_mp, n_dp = mesh.shape["segment"], mesh.shape["mp"], mesh.shape["dp"]

    def on_device(text_rows, durations, unit_targets, w_in, w_out, w_unit):
        micro, rows, width = text_rows.shape
        units = unit_targets.shape[1]
        hid_dev = w_in.shape[2]
        voc_dev = w_unit.shape[1]
        denom = float(micro * units * n_dp)
        kernel, scratch = make_kernel(
            n_seg, n_mp // 2, n_dp, micro // 2, 8, rows, width, hid_dev, voc_dev, units, denom
        )
        quarter = width // n_dp
        vmem = pl.BlockSpec(memory_space=pltpu.VMEM)
        loss, gin, gout, gun = pl.pallas_call(
            kernel,
            out_shape=(
                jax.ShapeDtypeStruct((1,), F32),
                jax.ShapeDtypeStruct((quarter, hid_dev), F32),
                jax.ShapeDtypeStruct((hid_dev, quarter), F32),
                jax.ShapeDtypeStruct((voc_dev, quarter), F32),
            ),
            in_specs=[pl.BlockSpec(memory_space=pl.ANY)] + [vmem] * 5,
            out_specs=(pl.BlockSpec(memory_space=pltpu.SMEM), vmem, vmem, vmem),
            scratch_shapes=scratch,
            compiler_params=pltpu.CompilerParams(
                collective_id=0, has_side_effects=True, vmem_limit_bytes=60 * 1024 * 1024
            ),
        )(
            text_rows, durations, unit_targets, w_in[0], w_out[0],
            jnp.transpose(w_unit),
        )
        return (loss, gin[None], gout[None], jnp.transpose(gun))

    placed = (
        P(None, "dp", None),
        P(None, "dp", None),
        P(None, "dp"),
        P("segment", None, "mp"),
        P("segment", "mp", None),
        P(None, ("segment", "mp")),
    )
    return jax.shard_map(
        on_device,
        mesh=mesh,
        in_specs=placed,
        out_specs=(
            P("dp"),
            P("segment", "dp", "mp"),
            P("segment", "mp", "dp"),
            P("dp", ("segment", "mp")),
        ),
        check_vma=False,
    )
```

```python
import jax
import jax.numpy as jnp
from jax import lax
from jax.experimental import pallas as pl
from jax.experimental.pallas import tpu as pltpu
from jax.sharding import PartitionSpec as P

MESH = pl.DeviceIdType.MESH
F32 = jnp.float32
BF16 = jnp.bfloat16

(
    G_FRS, G_FAG, G_FINY, G_FINZ, G_STAT, G_NRS, G_NY, G_NAG, G_BRS, G_BAG, G_TEXT, G_LOSS, G_SIBW,
) = range(13)
N_GROUPS = 13


def gelu_parts(pre_vals):
    coeff = 0.7978845608
    inner = coeff * (pre_vals + 0.044715 * pre_vals * pre_vals * pre_vals)
    tanh_val = jnp.tanh(inner)
    value = 0.5 * pre_vals * (1.0 + tanh_val)
    slope = 0.5 * (1.0 + tanh_val) + 0.5 * pre_vals * (1.0 - tanh_val * tanh_val) * coeff * (
        1.0 + 3.0 * 0.044715 * pre_vals * pre_vals
    )
    return (value, slope)


def row_scale(floats):
    return lax.rsqrt(jnp.mean(floats * floats, axis=-1, keepdims=True) + 1e-06)


def norm_back(floats, grads):
    scale = row_scale(floats)
    normal = floats * scale
    return scale * (grads - normal * jnp.mean(grads * normal, axis=-1, keepdims=True))


def nn(a, b):
    return jnp.dot(a, b, preferred_element_type=F32)


def nt(a, b):
    return lax.dot_general(a, b, (((1,), (1,)), ((), ())), preferred_element_type=F32)


def tn(a, b):
    return lax.dot_general(a, b, (((0,), (0,)), ((), ())), preferred_element_type=F32)


def make_kernel(n_seg, n_z, n_dp, micros, chunks, rows, width, hid_dev, voc_dev, units, denom):
    all_rows = micros * rows
    cut = all_rows // chunks
    per = chunks // micros
    col = width // n_z
    n_peer = n_seg * n_z
    quarter = width // n_dp
    blocks = n_z // n_dp

    def kernel(
        text, dur, tgt, w_in, w_out, w_unit,
        loss_o, gin_o, gout_o, gun_o,
        wi_sib, wo_sib, wu_sib,
        xbuf, normed, part, rsf, osh, hid, slo,
        fin, fn, lg, cnt, stb, dlb, partd, rsd, ysend, yrecv, dxb, dsh,
        dpre, partb, rsb, bsh,
        normed_sib, hidden_all, dx_all, dpre_sib, gu_f, gu_sib, gur_sib, gi_f,
        xs_u, xr_u, xs_i, xr_i,
        lvec, lown, lrcv,
        ssem, rsem, sib_s, sib_r, dp_s, dp_r, ex_s, ex_r,
    ):
        s = lax.axis_index("segment")
        mp = lax.axis_index("mp")
        d = lax.axis_index("dp")
        z = lax.div(mp, 2)
        c = lax.rem(mp, 2)
        sib = 2 * z + (1 - c)
        me = s * n_z + z
        last = n_seg - 1

        def cds(k):
            return pl.ds(pl.multiple_of(k * cut, cut), cut)

        def mds(m):
            return pl.ds(pl.multiple_of(m * rows, rows), rows)

        def whole(buf, where):
            return jnp.concatenate([buf[i, where, :] for i in range(n_z)], axis=-1)

        def columns(i):
            return slice(i * col, (i + 1) * col)

        def put(src, dst, a, b, where):
            pltpu.make_async_remote_copy(
                src_ref=src, dst_ref=dst, send_sem=a, recv_sem=b, device_id=where, device_id_type=MESH
            ).start()

        def drain(ref, sem):
            pltpu.make_async_copy(ref, ref, sem).wait()

        def span(start, stop, fn_of):
            def step(i, carry):
                fn_of(i)
                return carry

            lax.fori_loop(start, stop, step, 0)

        def over(n, fn_of):
            span(0, n, fn_of)

        def peers_z(fn_of):
            def step(i):
                side = 1 - 2 * lax.rem(i, 2)
                off = n_z // 2 + side * lax.div(i + 1, 2)
                fn_of(lax.rem(z + off, n_z))

            over(n_z - 1, step)

        barrier = pltpu.get_barrier_semaphore()

        def greet(where):
            pl.semaphore_signal(barrier, inc=1, device_id=where, device_id_type=MESH)

        peers_z(lambda z2: greet({"mp": 2 * z2 + c}))
        over(n_seg - 1, lambda i: greet({"segment": lax.rem(s + i + 1, n_seg)}))
        over(n_dp - 1, lambda i: greet({"dp": lax.rem(d + i + 1, n_dp)}))
        greet({"mp": sib})

        @pl.when(s == 0)
        def _():
            def load(k):
                for i in range(n_z):
                    pltpu.make_async_copy(
                        text.at[
                            micros * c + lax.div(k, per),
                            pl.ds(pl.multiple_of(lax.rem(k, per) * cut, cut), cut),
                            pl.ds(i * col, col),
                        ],
                        xbuf.at[i, cds(k)],
                        rsem.at[G_TEXT, k],
                    ).start()

            over(chunks, load)

        def count(k):
            lengths = dur[micros * c + k].astype(F32)
            lane = lax.broadcasted_iota(jnp.int32, (rows, rows), 1)
            sub = lax.broadcasted_iota(jnp.int32, (rows, rows), 0)
            tri = jnp.where(sub <= lane, 1.0, 0.0).astype(BF16)
            wide = jnp.broadcast_to(lengths, (8, rows)).astype(BF16)
            ends = nn(wide, tri)[0:1, :]
            starts = ends - lengths
            unit = lax.broadcasted_iota(jnp.int32, (units, rows), 0).astype(F32)
            onehot = jnp.where((starts <= unit) & (unit < ends), 1.0, 0.0).astype(BF16)
            target = tgt[pl.ds(micros * c + k, 1), :]
            ids = lax.broadcasted_iota(jnp.int32, (voc_dev, units), 0)
            for h, owner in ((0, mp), (1, sib)):
                first = (s * (2 * n_z) + owner) * voc_dev
                hits = jnp.where(ids + first == target, 1.0, 0.0).astype(BF16)
                cnt[k, h] = nn(hits, onehot)

        over(micros, count)
        pl.semaphore_wait(barrier, n_z - 1 + n_seg - 1 + n_dp - 1 + 1)

        put(w_in, wi_sib, ssem.at[G_SIBW, 0], rsem.at[G_SIBW, 0], {"mp": sib})
        put(w_out, wo_sib, ssem.at[G_SIBW, 1], rsem.at[G_SIBW, 1], {"mp": sib})
        put(w_unit, wu_sib, ssem.at[G_LOSS, 1], rsem.at[G_LOSS, 1], {"mp": sib})

        def scatter_z(buf, got, where, slot, group, k):
            own = got.at[slot, z]
            got[slot, z] = buf[z, where, :]
            peers_z(
                lambda z2: put(
                    buf.at[z2, where], own, ssem.at[group, k], rsem.at[group, k], {"mp": 2 * z2 + c}
                )
            )

        def in_plane(src, dst, group, k):
            peers_z(
                lambda z2: put(src, dst, ssem.at[group, k], rsem.at[group, k], {"mp": 2 * z2 + c})
            )

        def owned_sum(buf, k):
            total = buf[k, 0].astype(F32)
            for i in range(1, n_z):
                total = total + buf[k, i].astype(F32)
            return total

        def forward(k):
            @pl.when(s == 0)
            def _():
                drain(xbuf.at[:, cds(k)], rsem.at[G_TEXT, k])

            @pl.when(s > 0)
            def _():
                drain(xbuf.at[:, cds(k)], rsem.at[G_FAG, k])

            x = whole(xbuf, cds(k)).astype(F32)
            n = (x * row_scale(x)).astype(BF16)
            for i in range(n_z):
                normed[i, cds(k), :] = n[:, columns(i)]

            value, slope = gelu_parts(nn(n, w_in[...]))
            h0 = value.astype(BF16)
            hid[0, cds(k), :] = h0
            slo[0, cds(k), :] = slope
            acc = nn(h0, w_out[...])

            @pl.when(k == 0)
            def _():
                drain(wi_sib, rsem.at[G_SIBW, 0])
                drain(wo_sib, rsem.at[G_SIBW, 1])

            value, slope = gelu_parts(nn(n, wi_sib[...]))
            h1 = value.astype(BF16)
            hid[1, cds(k), :] = h1
            slo[1, cds(k), :] = slope
            acc = (acc + nn(h1, wo_sib[...])).astype(BF16)
            for i in range(n_z):
                part[i, cds(k), :] = acc[:, columns(i)]
            scatter_z(part, rsf, cds(k), k, G_FRS, k)

        def forward_end(k):
            drain(rsf.at[k, pl.ds(0, n_z - 1)], rsem.at[G_FRS, k])
            x = xbuf[z, cds(k), :].astype(F32)
            new = (x + owned_sum(rsf, k)).astype(BF16)
            osh[k] = new

            @pl.when(s < last)
            def _():
                def send(z2):
                    put(
                        osh.at[k], xbuf.at[z, cds(k)], ssem.at[G_FAG, k], rsem.at[G_FAG, k],
                        {"segment": s + 1, "mp": 2 * z2 + c},
                    )

                peers_z(send)
                send(z)

            @pl.when(s == last)
            def _():
                fin[z, cds(k), :] = new

                def send(y2):
                    put(
                        osh.at[k], fin.at[z, cds(k)], ssem.at[G_FINY, k], rsem.at[G_FINY, k],
                        {"segment": y2},
                    )

                over(n_seg - 1, send)
                in_plane(osh.at[k], fin.at[z, cds(k)], G_FINZ, k)

        def staged(first, second, start, stop):
            def step(i):
                @pl.when(i < chunks)
                def _():
                    first(i)

                @pl.when(i > 0)
                def _():
                    second(i - 1)

            span(start, stop, step)


        def relay(k):
            drain(fin.at[z, cds(k)], rsem.at[G_FINY, k])
            in_plane(fin.at[z, cds(k)], fin.at[z, cds(k)], G_FINZ, k)

        def logits(k):
            for j in range(per):
                drain(rsf.at[0, pl.ds(0, n_z - 1)], rsem.at[G_FINZ, k * per + j])
            x = whole(fin, mds(k)).astype(F32)
            n = (x * row_scale(x)).astype(BF16)
            fn[mds(k), :] = n
            a = nt(w_unit[...], n)
            b = nt(wu_sib[...], n)
            lg[k, 0] = a
            lg[k, 1] = b
            peak = jnp.maximum(jnp.max(a, axis=0, keepdims=True), jnp.max(b, axis=0, keepdims=True))
            total = jnp.sum(jnp.exp(a - peak), axis=0, keepdims=True) + jnp.sum(
                jnp.exp(b - peak), axis=0, keepdims=True
            )
            hit = jnp.sum(cnt[k, 0] * a, axis=0, keepdims=True) + jnp.sum(
                cnt[k, 1] * b, axis=0, keepdims=True
            )
            sub = lax.broadcasted_iota(jnp.int32, (8, rows), 0)
            stb[k, me] = jnp.where(sub == 0, peak, jnp.where(sub == 1, total, hit))

            def send(off):
                other = lax.rem(me + off + 1, n_peer)
                put(
                    stb.at[k, me], stb.at[k, me], ssem.at[G_STAT, k], rsem.at[G_STAT, k],
                    {"segment": lax.div(other, n_z), "mp": 2 * lax.rem(other, n_z) + c},
                )

            over(n_peer - 1, send)

        def dlogits(k):
            drain(stb.at[k, pl.ds(0, n_peer - 1)], rsem.at[G_STAT, k])
            every = stb[k]
            peaks = every[:, 0:1, :]
            peak = jnp.max(peaks, axis=0)
            total = jnp.sum(every[:, 1:2, :] * jnp.exp(peaks - peak[None]), axis=0)
            hit = jnp.sum(every[:, 2:3, :], axis=0)
            lse = peak + jnp.log(total)
            lengths = dur[micros * c + k].astype(F32)
            lvec[0:1, :] += lengths * lse - hit
            acc = None
            for h, w in ((0, w_unit), (1, wu_sib)):
                grad = (lengths * jnp.exp(lg[k, h] - lse) - cnt[k, h]) * (1.0 / denom)
                grad = grad.astype(BF16)
                dlb[h, k] = grad
                term = tn(grad, w[...])
                acc = term if acc is None else acc + term
            x = whole(fin, mds(k)).astype(F32)
            acc = norm_back(x, acc).astype(BF16)
            for i in range(n_z):
                partd[i, mds(k), :] = acc[:, columns(i)]
            span(k * per, (k + 1) * per, lambda j: scatter_z(partd, rsd, cds(j), j, G_NRS, j))

        def norm_sum(k):
            drain(rsd.at[k, pl.ds(0, n_z - 1)], rsem.at[G_NRS, k])
            ysend[k] = owned_sum(rsd, k).astype(BF16)

            @pl.when(s < last)
            def _():
                put(ysend.at[k], yrecv.at[k, s], ssem.at[G_NY, k], rsem.at[G_NY, k], {"segment": last})

        def norm_end(k):
            drain(yrecv.at[k], rsem.at[G_NY, k])
            total = ysend[k].astype(F32)
            for i in range(n_seg - 1):
                total = total + yrecv[k, i].astype(F32)
            grad = total.astype(BF16)
            dsh[k] = grad
            dxb[z, cds(k), :] = grad
            in_plane(dsh.at[k], dxb.at[z, cds(k)], G_NAG, k)

        def dp_send(xs, xr, g):
            def step(off):
                d2 = lax.rem(d + off + 1, n_dp)
                put(xs.at[d2], xr.at[d], dp_s.at[g], dp_r.at[g], {"dp": d2})

            over(n_dp - 1, step)

        def dp_out(own, xr, g, out):
            drain(xr.at[pl.ds(0, n_dp - 1)], dp_r.at[g])
            total = own
            for off in range(1, n_dp):
                total = total + xr[lax.rem(d + off, n_dp)].astype(F32)
            out[...] = total

        def unit_grad():
            lown[...] = jnp.broadcast_to(jnp.sum(lvec[...], keepdims=True), lown.shape)
            put(lown, lrcv, ssem.at[G_LOSS, 0], rsem.at[G_LOSS, 0], {"mp": sib})
            for h in (1, 0):
                total = nn(dlb[h, 0], fn[pl.ds(0, rows), :])
                for k in range(1, micros):
                    total = total + nn(dlb[h, k], fn[pl.ds(k * rows, rows), :])
                for q in range(n_dp):
                    piece = total[:, q * quarter : (q + 1) * quarter]
                    if h == 1:
                        gu_sib[q] = piece.astype(BF16)
                    else:
                        gu_f[q] = piece
                if h == 1:
                    put(gu_sib, gur_sib, sib_s.at[0], sib_r.at[0], {"mp": sib})
            drain(gur_sib, sib_r.at[0])

            def unit_sum(q):
                total = gu_f[q] + gur_sib[q].astype(F32)
                gu_f[q] = total
                xs_u[q] = total.astype(BF16)

            over(n_dp, unit_sum)
            dp_send(xs_u, xr_u, 0)

        def backward(k):
            @pl.when(s == last)
            def _():
                drain(rsd.at[0, pl.ds(0, n_z - 1)], rsem.at[G_NAG, k])

            @pl.when(s < last)
            def _():
                drain(dxb.at[:, cds(k)], rsem.at[G_BAG, k])

            g = whole(dxb, cds(k))
            p0 = (nt(g, w_out[...]) * slo[0, cds(k), :]).astype(BF16)
            dpre[0, cds(k), :] = p0
            p1 = (nt(g, wo_sib[...]) * slo[1, cds(k), :]).astype(BF16)
            dpre[1, cds(k), :] = p1
            put(dpre.at[1, cds(k)], dpre_sib.at[cds(k)], ex_s.at[3], ex_r.at[3], {"mp": sib})

            def share(off):
                other = lax.rem(2 * d + c + off, 2 * n_dp)
                d2 = lax.div(other, 2)
                put(
                    dxb.at[pl.ds(d2 * blocks, blocks), cds(k)], dx_all.at[2 * d + c, :, cds(k)],
                    ex_s.at[2], ex_r.at[2], {"dp": d2, "mp": 2 * z + lax.rem(other, 2)},
                )

            span(1, 2 * n_dp, share)

            @pl.when(s > 0)
            def _():
                x = whole(xbuf, cds(k)).astype(F32)
                acc = norm_back(x, nt(p0, w_in[...]) + nt(p1, wi_sib[...])).astype(BF16)
                for i in range(n_z):
                    partb[i, cds(k), :] = acc[:, columns(i)]
                scatter_z(partb, rsb, cds(k), k, G_BRS, k)

        def backward_end(k):
            @pl.when(s > 0)
            def _():
                drain(rsb.at[k, pl.ds(0, n_z - 1)], rsem.at[G_BRS, k])
                bsh[k] = (dxb[z, cds(k), :].astype(F32) + owned_sum(rsb, k)).astype(BF16)

                def send(z2):
                    put(
                        bsh.at[k], dxb.at[z, cds(k)], ssem.at[G_BAG, k], rsem.at[G_BAG, k],
                        {"segment": s - 1, "mp": 2 * z2 + c},
                    )

                peers_z(send)
                send(z)

        def share_hidden():
            put(normed, normed_sib, ex_s.at[0], ex_r.at[0], {"mp": sib})

            def step(off):
                other = lax.rem(2 * d + c + off, 2 * n_dp)
                c2 = lax.rem(other, 2)
                put(
                    hid.at[lax.rem(c + c2, 2)], hidden_all.at[2 * d + c],
                    ex_s.at[1], ex_r.at[1], {"dp": lax.div(other, 2), "mp": 2 * z + c2},
                )

            span(1, 2 * n_dp, step)

        early = per + per // 2
        staged(forward, forward_end, 0, early + 1)
        drain(wu_sib, rsem.at[G_LOSS, 1])
        lvec[...] = jnp.zeros_like(lvec)

        @pl.when(s == last)
        def _():
            logits(0)

        staged(forward, forward_end, early + 1, chunks + 1)

        @pl.when(s < last)
        def _():
            share_hidden()
            over(early, relay)
            logits(0)
            span(early, chunks, relay)

        dlogits(0)
        logits(1)

        @pl.when(s < last)
        def _():
            over(per - 1, norm_sum)
            dlogits(1)
            span(per - 1, chunks, norm_sum)
            unit_grad()
            staged(backward, backward_end, 0, chunks + 1)

        @pl.when(s == last)
        def _():
            over(per - 1, norm_sum)
            norm_end(0)
            dlogits(1)
            norm_sum(per - 1)
            span(1, per, norm_end)

            share_hidden()

            def first_half(i):
                backward(i)
                norm_sum(per + i)

            over(per, first_half)

            def second_half(i):
                norm_end(per + i)
                backward_end(i)

            over(per, second_half)
            span(per, chunks, backward)
            span(per, chunks, backward_end)
            unit_grad()

        drain(dpre_sib, ex_r.at[3])
        drain(normed_sib, ex_r.at[0])

        def in_quarter(q):
            own = jnp.concatenate([normed[q * blocks + i] for i in range(blocks)], axis=-1)
            other = jnp.concatenate([normed_sib[q * blocks + i] for i in range(blocks)], axis=-1)
            return tn(own, dpre[0]) + tn(other, dpre_sib[...])

        def in_send(off):
            d2 = lax.rem(d + off + 1, n_dp)
            xs_i[d2] = in_quarter(d2).astype(BF16)
            put(xs_i.at[d2], xr_i.at[d], dp_s.at[1], dp_r.at[1], {"dp": d2})

        over(n_dp - 1, in_send)
        gi_f[...] = in_quarter(d)

        drain(hidden_all.at[pl.ds(0, 2 * n_dp - 1)], ex_r.at[1])
        drain(dx_all.at[pl.ds(0, 2 * n_dp - 1)], ex_r.at[2])
        own_dx = jnp.concatenate([dxb[d * blocks + i] for i in range(blocks)], axis=-1)
        gout_o[...] = tn(hid[0], own_dx)

        def out_term(off):
            other = lax.rem(2 * d + c + off, 2 * n_dp)
            got = jnp.concatenate([dx_all[other, i] for i in range(blocks)], axis=-1)
            gout_o[...] += tn(hidden_all[other], got)

        span(1, 2 * n_dp, out_term)

        dp_out(gu_f[d], xr_u, 0, gun_o)
        drain(lrcv, rsem.at[G_LOSS, 0])
        loss_o[0] = jnp.max(lown[...] + lrcv[...]) * (1.0 / denom)
        dp_out(gi_f[...], xr_i, 1, gin_o)

        drain(w_in, ssem.at[G_SIBW, 0])
        drain(w_out, ssem.at[G_SIBW, 1])
        drain(w_unit, ssem.at[G_LOSS, 1])
        drain(lown, ssem.at[G_LOSS, 0])
        drain(gu_sib, sib_s.at[0])
        drain(xs_u.at[pl.ds(0, n_dp - 1)], dp_s.at[0])
        drain(xs_i.at[pl.ds(0, n_dp - 1)], dp_s.at[1])
        drain(normed, ex_s.at[0])
        drain(hidden_all.at[pl.ds(0, 2 * n_dp - 1)], ex_s.at[1])
        drain(dx_all.at[pl.ds(0, 2 * n_dp - 1)], ex_s.at[2])
        drain(dpre_sib, ex_s.at[3])

        def finish(k):
            part_of = rsf.at[0, pl.ds(0, n_z - 1)]
            drain(part_of, ssem.at[G_FRS, k])
            drain(part_of, ssem.at[G_FINZ, k])

            drain(part_of, ssem.at[G_NRS, k])

            @pl.when(s < last)
            def _():
                drain(rsf.at[0], ssem.at[G_FAG, k])
                drain(ysend.at[k], ssem.at[G_NY, k])

            @pl.when(s == last)
            def _():
                drain(osh.at[pl.ds(0, n_seg - 1)], ssem.at[G_FINY, k])
                drain(part_of, ssem.at[G_NAG, k])

            @pl.when(s > 0)
            def _():
                drain(part_of, ssem.at[G_BRS, k])
                drain(rsf.at[0], ssem.at[G_BAG, k])

        def finish_micro(k):
            drain(stb.at[k, pl.ds(0, n_peer - 1)], ssem.at[G_STAT, k])

        over(chunks, finish)
        over(micros, finish_micro)

    vm = pltpu.VMEM
    lines = (n_z, all_rows, col)
    shard = (chunks, cut, col)
    scatter = (chunks, n_z, cut, col)
    scratch = [
        vm((width, hid_dev), BF16), vm((hid_dev, width), BF16), vm((voc_dev, width), BF16),
        vm(lines, BF16), vm(lines, BF16), vm(lines, BF16),
        vm(scatter, BF16), vm(shard, BF16), vm((2, all_rows, hid_dev), BF16), vm((2, all_rows, hid_dev), F32),
        vm(lines, BF16), vm((all_rows, width), BF16),
        vm((micros, 2, voc_dev, rows), F32), vm((micros, 2, voc_dev, rows), F32),
        vm((micros, n_peer, 8, rows), F32), vm((2, micros, voc_dev, rows), BF16),
        vm(lines, BF16), vm(scatter, BF16), vm(shard, BF16),
        vm((chunks, n_seg - 1, cut, col), BF16), vm(lines, BF16), vm(shard, BF16),
        vm((2, all_rows, hid_dev), BF16), vm(lines, BF16), vm(scatter, BF16), vm(shard, BF16),
        vm(lines, BF16), vm((2 * n_dp, all_rows, hid_dev), BF16),
        vm((2 * n_dp, n_z // n_dp, all_rows, col), BF16), vm((all_rows, hid_dev), BF16),
        vm((n_dp, voc_dev, quarter), F32), vm((n_dp, voc_dev, quarter), BF16), vm((n_dp, voc_dev, quarter), BF16),
        vm((quarter, hid_dev), F32),
        vm((n_dp, voc_dev, quarter), BF16), vm((n_dp, voc_dev, quarter), BF16),
        vm((n_dp, quarter, hid_dev), BF16), vm((n_dp, quarter, hid_dev), BF16),
        vm((8, rows), F32), vm((8, 128), F32), vm((8, 128), F32),
        pltpu.SemaphoreType.DMA((N_GROUPS, chunks)), pltpu.SemaphoreType.DMA((N_GROUPS, chunks)),
        pltpu.SemaphoreType.DMA((1,)), pltpu.SemaphoreType.DMA((1,)),
        pltpu.SemaphoreType.DMA((2,)), pltpu.SemaphoreType.DMA((2,)),
        pltpu.SemaphoreType.DMA((4,)), pltpu.SemaphoreType.DMA((4,)),
    ]
    return kernel, scratch


def solution(mesh):
    n_seg, n_mp, n_dp = mesh.shape["segment"], mesh.shape["mp"], mesh.shape["dp"]

    def on_device(text_rows, durations, unit_targets, w_in, w_out, w_unit):
        micro, rows, width = text_rows.shape
        units = unit_targets.shape[1]
        hid_dev = w_in.shape[2]
        voc_dev = w_unit.shape[1]
        denom = float(micro * units * n_dp)
        kernel, scratch = make_kernel(
            n_seg, n_mp // 2, n_dp, micro // 2, 8, rows, width, hid_dev, voc_dev, units, denom
        )
        quarter = width // n_dp
        vmem = pl.BlockSpec(memory_space=pltpu.VMEM)
        loss, gin, gout, gun = pl.pallas_call(
            kernel,
            out_shape=(
                jax.ShapeDtypeStruct((1,), F32),
                jax.ShapeDtypeStruct((quarter, hid_dev), F32),
                jax.ShapeDtypeStruct((hid_dev, quarter), F32),
                jax.ShapeDtypeStruct((voc_dev, quarter), F32),
            ),
            in_specs=[pl.BlockSpec(memory_space=pl.ANY)] + [vmem] * 5,
            out_specs=(pl.BlockSpec(memory_space=pltpu.SMEM), vmem, vmem, vmem),
            scratch_shapes=scratch,
            compiler_params=pltpu.CompilerParams(
                collective_id=0, has_side_effects=True, vmem_limit_bytes=60 * 1024 * 1024
            ),
        )(
            text_rows, durations, unit_targets, w_in[0], w_out[0],
            jnp.transpose(w_unit),
        )
        return (loss, gin[None], gout[None], jnp.transpose(gun))

    placed = (
        P(None, "dp", None),
        P(None, "dp", None),
        P(None, "dp"),
        P("segment", None, "mp"),
        P("segment", "mp", None),
        P(None, ("segment", "mp")),
    )
    return jax.shard_map(
        on_device,
        mesh=mesh,
        in_specs=placed,
        out_specs=(
            P("dp"),
            P("segment", "dp", "mp"),
            P("segment", "mp", "dp"),
            P("dp", ("segment", "mp")),
        ),
        check_vma=False,
    )
```

```python
import jax
import jax.numpy as jnp
from jax import lax
from jax.experimental import pallas as pl
from jax.experimental.pallas import tpu as pltpu
from jax.sharding import PartitionSpec as P

MESH = pl.DeviceIdType.MESH
F32 = jnp.float32
BF16 = jnp.bfloat16

(
    G_FRS, G_FAG, G_FINY, G_FINZ, G_STAT, G_NRS, G_NY, G_NAG, G_BRS, G_BAG, G_TEXT, G_LOSS, G_SIBW,
) = range(13)
N_GROUPS = 13


def gelu_parts(pre_vals):
    coeff = 0.7978845608
    inner = coeff * (pre_vals + 0.044715 * pre_vals * pre_vals * pre_vals)
    tanh_val = jnp.tanh(inner)
    value = 0.5 * pre_vals * (1.0 + tanh_val)
    slope = 0.5 * (1.0 + tanh_val) + 0.5 * pre_vals * (1.0 - tanh_val * tanh_val) * coeff * (
        1.0 + 3.0 * 0.044715 * pre_vals * pre_vals
    )
    return (value, slope)


def row_scale(floats):
    return lax.rsqrt(jnp.mean(floats * floats, axis=-1, keepdims=True) + 1e-06)


def norm_back(floats, grads):
    scale = row_scale(floats)
    normal = floats * scale
    return scale * (grads - normal * jnp.mean(grads * normal, axis=-1, keepdims=True))


def nn(a, b):
    return jnp.dot(a, b, preferred_element_type=F32)


def nt(a, b):
    return lax.dot_general(a, b, (((1,), (1,)), ((), ())), preferred_element_type=F32)


def tn(a, b):
    return lax.dot_general(a, b, (((0,), (0,)), ((), ())), preferred_element_type=F32)


def make_kernel(n_seg, n_z, n_dp, micros, chunks, rows, width, hid_dev, voc_dev, units, denom):
    all_rows = micros * rows
    cut = all_rows // chunks
    per = chunks // micros
    col = width // n_z
    n_peer = n_seg * n_z
    quarter = width // n_dp
    blocks = n_z // n_dp

    def kernel(
        text, dur, tgt, w_in, w_out, w_unit,
        loss_o, gin_o, gout_o, gun_o,
        wi_sib, wo_sib, wu_sib,
        xbuf, normed, part, rsf, osh, hid, slo,
        fin, fn, lg, cnt, stb, dlb, partd, rsd, ysend, yrecv, dxb, dsh,
        dpre, partb, rsb, bsh,
        normed_sib, hidden_all, dx_all, dpre_sib, gu_f, gu_sib, gur_sib, gi_f,
        xs_u, xr_u, xs_i, xr_i,
        lvec, lown, lrcv,
        ssem, rsem, sib_s, sib_r, dp_s, dp_r, ex_s, ex_r,
    ):
        s = lax.axis_index("segment")
        mp = lax.axis_index("mp")
        d = lax.axis_index("dp")
        z = lax.div(mp, 2)
        c = lax.rem(mp, 2)
        sib = 2 * z + (1 - c)
        me = s * n_z + z
        last = n_seg - 1
        hub = n_seg - 2

        def cds(k):
            return pl.ds(pl.multiple_of(k * cut, cut), cut)

        def mds(m):
            return pl.ds(pl.multiple_of(m * rows, rows), rows)

        def whole(buf, where):
            return jnp.concatenate([buf[i, where, :] for i in range(n_z)], axis=-1)

        def columns(i):
            return slice(i * col, (i + 1) * col)

        def put(src, dst, a, b, where):
            pltpu.make_async_remote_copy(
                src_ref=src, dst_ref=dst, send_sem=a, recv_sem=b, device_id=where, device_id_type=MESH
            ).start()

        def drain(ref, sem):
            pltpu.make_async_copy(ref, ref, sem).wait()

        def span(start, stop, fn_of):
            def step(i, carry):
                fn_of(i)
                return carry

            lax.fori_loop(start, stop, step, 0)

        def over(n, fn_of):
            span(0, n, fn_of)

        def peers_z(fn_of):
            def step(i):
                side = 1 - 2 * lax.rem(i, 2)
                off = n_z // 2 + side * lax.div(i + 1, 2)
                fn_of(lax.rem(z + off, n_z))

            over(n_z - 1, step)

        barrier = pltpu.get_barrier_semaphore()

        def greet(where):
            pl.semaphore_signal(barrier, inc=1, device_id=where, device_id_type=MESH)

        peers_z(lambda z2: greet({"mp": 2 * z2 + c}))
        over(n_seg - 1, lambda i: greet({"segment": lax.rem(s + i + 1, n_seg)}))
        over(n_dp - 1, lambda i: greet({"dp": lax.rem(d + i + 1, n_dp)}))
        greet({"mp": sib})

        @pl.when(s == 0)
        def _():
            def load(k):
                for i in range(n_z):
                    pltpu.make_async_copy(
                        text.at[
                            micros * c + lax.div(k, per),
                            pl.ds(pl.multiple_of(lax.rem(k, per) * cut, cut), cut),
                            pl.ds(i * col, col),
                        ],
                        xbuf.at[i, cds(k)],
                        rsem.at[G_TEXT, k],
                    ).start()

            over(chunks, load)

        def count(k):
            lengths = dur[micros * c + k].astype(F32)
            lane = lax.broadcasted_iota(jnp.int32, (rows, rows), 1)
            sub = lax.broadcasted_iota(jnp.int32, (rows, rows), 0)
            tri = jnp.where(sub <= lane, 1.0, 0.0).astype(BF16)
            wide = jnp.broadcast_to(lengths, (8, rows)).astype(BF16)
            ends = nn(wide, tri)[0:1, :]
            starts = ends - lengths
            unit = lax.broadcasted_iota(jnp.int32, (units, rows), 0).astype(F32)
            onehot = jnp.where((starts <= unit) & (unit < ends), 1.0, 0.0).astype(BF16)
            target = tgt[pl.ds(micros * c + k, 1), :]
            ids = lax.broadcasted_iota(jnp.int32, (voc_dev, units), 0)
            for h, owner in ((0, mp), (1, sib)):
                first = (s * (2 * n_z) + owner) * voc_dev
                hits = jnp.where(ids + first == target, 1.0, 0.0).astype(BF16)
                cnt[k, h] = nn(hits, onehot)

        over(micros, count)
        pl.semaphore_wait(barrier, n_z - 1 + n_seg - 1 + n_dp - 1 + 1)

        put(w_in, wi_sib, ssem.at[G_SIBW, 0], rsem.at[G_SIBW, 0], {"mp": sib})
        put(w_out, wo_sib, ssem.at[G_SIBW, 1], rsem.at[G_SIBW, 1], {"mp": sib})
        put(w_unit, wu_sib, ssem.at[G_LOSS, 1], rsem.at[G_LOSS, 1], {"mp": sib})

        def scatter_z(buf, got, where, slot, group, k):
            own = got.at[slot, z]
            got[slot, z] = buf[z, where, :]
            peers_z(
                lambda z2: put(
                    buf.at[z2, where], own, ssem.at[group, k], rsem.at[group, k], {"mp": 2 * z2 + c}
                )
            )

        def in_plane(src, dst, group, k):
            peers_z(
                lambda z2: put(src, dst, ssem.at[group, k], rsem.at[group, k], {"mp": 2 * z2 + c})
            )

        def owned_sum(buf, k):
            total = buf[k, 0].astype(F32)
            for i in range(1, n_z):
                total = total + buf[k, i].astype(F32)
            return total

        def forward(k):
            @pl.when(s == 0)
            def _():
                drain(xbuf.at[:, cds(k)], rsem.at[G_TEXT, k])

            @pl.when(s > 0)
            def _():
                drain(xbuf.at[:, cds(k)], rsem.at[G_FAG, k])

            x = whole(xbuf, cds(k)).astype(F32)
            n = (x * row_scale(x)).astype(BF16)
            for i in range(n_z):
                normed[i, cds(k), :] = n[:, columns(i)]

            value, slope = gelu_parts(nn(n, w_in[...]))
            h0 = value.astype(BF16)
            hid[0, cds(k), :] = h0
            slo[0, cds(k), :] = slope
            acc = nn(h0, w_out[...])

            @pl.when(k == 0)
            def _():
                drain(wi_sib, rsem.at[G_SIBW, 0])
                drain(wo_sib, rsem.at[G_SIBW, 1])

            value, slope = gelu_parts(nn(n, wi_sib[...]))
            h1 = value.astype(BF16)
            hid[1, cds(k), :] = h1
            slo[1, cds(k), :] = slope
            acc = (acc + nn(h1, wo_sib[...])).astype(BF16)
            for i in range(n_z):
                part[i, cds(k), :] = acc[:, columns(i)]
            scatter_z(part, rsf, cds(k), k, G_FRS, k)

        def forward_end(k):
            drain(rsf.at[k, pl.ds(0, n_z - 1)], rsem.at[G_FRS, k])
            x = xbuf[z, cds(k), :].astype(F32)
            new = (x + owned_sum(rsf, k)).astype(BF16)
            osh[k] = new

            @pl.when(s < last)
            def _():
                def send(z2):
                    put(
                        osh.at[k], xbuf.at[z, cds(k)], ssem.at[G_FAG, k], rsem.at[G_FAG, k],
                        {"segment": s + 1, "mp": 2 * z2 + c},
                    )

                peers_z(send)
                send(z)

            @pl.when(s == last)
            def _():
                fin[z, cds(k), :] = new

                def send(y2):
                    put(
                        osh.at[k], fin.at[z, cds(k)], ssem.at[G_FINY, k], rsem.at[G_FINY, k],
                        {"segment": y2},
                    )

                over(n_seg - 1, send)
                in_plane(osh.at[k], fin.at[z, cds(k)], G_FINZ, k)

        def staged(first, second, start, stop):
            def step(i):
                @pl.when(i < chunks)
                def _():
                    first(i)

                @pl.when(i > 0)
                def _():
                    second(i - 1)

            span(start, stop, step)


        def relay(k):
            drain(fin.at[z, cds(k)], rsem.at[G_FINY, k])
            in_plane(fin.at[z, cds(k)], fin.at[z, cds(k)], G_FINZ, k)

        def logits(k):
            for j in range(per):
                drain(rsf.at[0, pl.ds(0, n_z - 1)], rsem.at[G_FINZ, k * per + j])
            x = whole(fin, mds(k)).astype(F32)
            n = (x * row_scale(x)).astype(BF16)
            fn[mds(k), :] = n
            a = nt(w_unit[...], n)
            b = nt(wu_sib[...], n)
            lg[k, 0] = a
            lg[k, 1] = b
            peak = jnp.maximum(jnp.max(a, axis=0, keepdims=True), jnp.max(b, axis=0, keepdims=True))
            total = jnp.sum(jnp.exp(a - peak), axis=0, keepdims=True) + jnp.sum(
                jnp.exp(b - peak), axis=0, keepdims=True
            )
            hit = jnp.sum(cnt[k, 0] * a, axis=0, keepdims=True) + jnp.sum(
                cnt[k, 1] * b, axis=0, keepdims=True
            )
            sub = lax.broadcasted_iota(jnp.int32, (4, rows), 0)
            stb[k, me] = jnp.where(sub == 0, peak, jnp.where(sub == 1, total, hit))

            def send(off):
                other = lax.rem(me + off + 1, n_peer)
                put(
                    stb.at[k, me], stb.at[k, me], ssem.at[G_STAT, k], rsem.at[G_STAT, k],
                    {"segment": lax.div(other, n_z), "mp": 2 * lax.rem(other, n_z) + c},
                )

            over(n_peer - 1, send)

        def dlogits(k):
            drain(stb.at[k, pl.ds(0, n_peer - 1)], rsem.at[G_STAT, k])
            every = stb[k]
            peaks = every[:, 0:1, :]
            peak = jnp.max(peaks, axis=0)
            total = jnp.sum(every[:, 1:2, :] * jnp.exp(peaks - peak[None]), axis=0)
            hit = jnp.sum(every[:, 2:3, :], axis=0)
            lse = peak + jnp.log(total)
            lengths = dur[micros * c + k].astype(F32)
            lvec[0:1, :] += lengths * lse - hit
            acc = None
            for h, w in ((0, w_unit), (1, wu_sib)):
                grad = (lengths * jnp.exp(lg[k, h] - lse) - cnt[k, h]) * (1.0 / denom)
                grad = grad.astype(BF16)
                dlb[h, k] = grad
                term = tn(grad, w[...])
                acc = term if acc is None else acc + term
            x = whole(fin, mds(k)).astype(F32)
            acc = norm_back(x, acc).astype(BF16)
            for i in range(n_z):
                partd[i, mds(k), :] = acc[:, columns(i)]
            span(k * per, (k + 1) * per, lambda j: scatter_z(partd, rsd, cds(j), j, G_NRS, j))

        def norm_sum(k):
            drain(rsd.at[k, pl.ds(0, n_z - 1)], rsem.at[G_NRS, k])
            ysend[k] = owned_sum(rsd, k).astype(BF16)

            @pl.when(s != hub)
            def _():
                slot = jnp.minimum(s, hub)
                put(ysend.at[k], yrecv.at[k, slot], ssem.at[G_NY, k], rsem.at[G_NY, k], {"segment": hub})

        def norm_end(k):
            drain(yrecv.at[k], rsem.at[G_NY, k])
            total = ysend[k].astype(F32)
            for i in range(n_seg - 1):
                total = total + yrecv[k, i].astype(F32)
            dsh[k] = total.astype(BF16)

            def send(z2):
                put(
                    dsh.at[k], dxb.at[z, cds(k)], ssem.at[G_NAG, k], rsem.at[G_NAG, k],
                    {"segment": last, "mp": 2 * z2 + c},
                )

            peers_z(send)
            send(z)

        def dp_send(xs, xr, g):
            def step(off):
                d2 = lax.rem(d + off + 1, n_dp)
                put(xs.at[d2], xr.at[d], dp_s.at[g], dp_r.at[g], {"dp": d2})

            over(n_dp - 1, step)

        def dp_out(own, xr, g, out):
            drain(xr.at[pl.ds(0, n_dp - 1)], dp_r.at[g])
            total = own
            for off in range(1, n_dp):
                total = total + xr[lax.rem(d + off, n_dp)].astype(F32)
            out[...] = total

        def unit_grad():
            lown[...] = jnp.broadcast_to(jnp.sum(lvec[...], keepdims=True), lown.shape)
            put(lown, lrcv, ssem.at[G_LOSS, 0], rsem.at[G_LOSS, 0], {"mp": sib})
            for h in (1, 0):
                total = nn(dlb[h, 0], fn[pl.ds(0, rows), :])
                for k in range(1, micros):
                    total = total + nn(dlb[h, k], fn[pl.ds(k * rows, rows), :])
                for q in range(n_dp):
                    piece = total[:, q * quarter : (q + 1) * quarter]
                    if h == 1:
                        gu_sib[q] = piece.astype(BF16)
                    else:
                        gu_f[q] = piece
                if h == 1:
                    put(gu_sib, gur_sib, sib_s.at[0], sib_r.at[0], {"mp": sib})
            drain(gur_sib, sib_r.at[0])

            def unit_sum(q):
                total = gu_f[q] + gur_sib[q].astype(F32)
                gu_f[q] = total
                xs_u[q] = total.astype(BF16)

            over(n_dp, unit_sum)
            dp_send(xs_u, xr_u, 0)

        def backward(k):
            @pl.when(s == last)
            def _():
                drain(dxb.at[:, cds(k)], rsem.at[G_NAG, k])

            @pl.when(s < last)
            def _():
                drain(dxb.at[:, cds(k)], rsem.at[G_BAG, k])

            g = whole(dxb, cds(k))
            p0 = (nt(g, w_out[...]) * slo[0, cds(k), :]).astype(BF16)
            dpre[0, cds(k), :] = p0
            p1 = (nt(g, wo_sib[...]) * slo[1, cds(k), :]).astype(BF16)
            dpre[1, cds(k), :] = p1

            @pl.when(s > 0)
            def _():
                x = whole(xbuf, cds(k)).astype(F32)
                acc = norm_back(x, nt(p0, w_in[...]) + nt(p1, wi_sib[...])).astype(BF16)
                for i in range(n_z):
                    partb[i, cds(k), :] = acc[:, columns(i)]
                scatter_z(partb, rsb, cds(k), k, G_BRS, k)

            put(dpre.at[1, cds(k)], dpre_sib.at[cds(k)], ex_s.at[3], ex_r.at[3], {"mp": sib})

            def share(off):
                other = lax.rem(2 * d + c + off, 2 * n_dp)
                d2 = lax.div(other, 2)
                put(
                    dxb.at[pl.ds(d2 * blocks, blocks), cds(k)], dx_all.at[2 * d + c, :, cds(k)],
                    ex_s.at[2], ex_r.at[2], {"dp": d2, "mp": 2 * z + lax.rem(other, 2)},
                )

            span(1, 2 * n_dp, share)

        def backward_end(k):
            @pl.when(s > 0)
            def _():
                drain(rsb.at[k, pl.ds(0, n_z - 1)], rsem.at[G_BRS, k])
                bsh[k] = (dxb[z, cds(k), :].astype(F32) + owned_sum(rsb, k)).astype(BF16)

                def send(z2):
                    put(
                        bsh.at[k], dxb.at[z, cds(k)], ssem.at[G_BAG, k], rsem.at[G_BAG, k],
                        {"segment": s - 1, "mp": 2 * z2 + c},
                    )

                peers_z(send)
                send(z)

        def share_hidden():
            put(normed, normed_sib, ex_s.at[0], ex_r.at[0], {"mp": sib})

            def step(off):
                other = lax.rem(2 * d + c + off, 2 * n_dp)
                c2 = lax.rem(other, 2)
                put(
                    hid.at[lax.rem(c + c2, 2)], hidden_all.at[2 * d + c],
                    ex_s.at[1], ex_r.at[1], {"dp": lax.div(other, 2), "mp": 2 * z + c2},
                )

            span(1, 2 * n_dp, step)

        early = per + per // 2
        staged(forward, forward_end, 0, early + 1)
        drain(wu_sib, rsem.at[G_LOSS, 1])
        lvec[...] = jnp.zeros_like(lvec)

        @pl.when(s == last)
        def _():
            logits(0)

        staged(forward, forward_end, early + 1, chunks + 1)

        @pl.when(s < last)
        def _():
            over(early, relay)
            logits(0)
            span(early, chunks, relay)
            share_hidden()

        dlogits(0)
        logits(1)

        over(per - 1, norm_sum)

        @pl.when(s == hub)
        def _():
            norm_end(0)

        dlogits(1)
        norm_sum(per - 1)

        @pl.when(s == hub)
        def _():
            span(1, per, norm_end)

        @pl.when(s < last)
        def _():
            def late(i):
                @pl.when(i < chunks)
                def _():
                    norm_sum(i)

                @pl.when((s == hub) & (i >= per + 2))
                def _():
                    norm_end(i - 2)

            span(per, chunks + 2, late)
            unit_grad()
            staged(backward, backward_end, 0, chunks + 1)

        @pl.when(s == last)
        def _():
            share_hidden()

            def first_half(i):
                backward(i)
                norm_sum(per + i)

            over(per, first_half)
            over(per, backward_end)
            span(per, chunks, backward)
            span(per, chunks, backward_end)
            unit_grad()

        drain(dpre_sib, ex_r.at[3])
        drain(normed_sib, ex_r.at[0])

        def in_quarter(q):
            own = jnp.concatenate([normed[q * blocks + i] for i in range(blocks)], axis=-1)
            other = jnp.concatenate([normed_sib[q * blocks + i] for i in range(blocks)], axis=-1)
            return tn(own, dpre[0]) + tn(other, dpre_sib[...])

        def in_send(off):
            d2 = lax.rem(d + off + 1, n_dp)
            xs_i[d2] = in_quarter(d2).astype(BF16)
            put(xs_i.at[d2], xr_i.at[d], dp_s.at[1], dp_r.at[1], {"dp": d2})

        over(n_dp - 1, in_send)
        gi_f[...] = in_quarter(d)

        drain(hidden_all.at[pl.ds(0, 2 * n_dp - 1)], ex_r.at[1])
        drain(dx_all.at[pl.ds(0, 2 * n_dp - 1)], ex_r.at[2])
        own_dx = jnp.concatenate([dxb[d * blocks + i] for i in range(blocks)], axis=-1)
        gout_o[...] = tn(hid[0], own_dx)

        def out_term(off):
            other = lax.rem(2 * d + c + off, 2 * n_dp)
            got = jnp.concatenate([dx_all[other, i] for i in range(blocks)], axis=-1)
            gout_o[...] += tn(hidden_all[other], got)

        span(1, 2 * n_dp, out_term)

        dp_out(gu_f[d], xr_u, 0, gun_o)
        drain(lrcv, rsem.at[G_LOSS, 0])
        loss_o[0] = jnp.max(lown[...] + lrcv[...]) * (1.0 / denom)
        dp_out(gi_f[...], xr_i, 1, gin_o)

        drain(w_in, ssem.at[G_SIBW, 0])
        drain(w_out, ssem.at[G_SIBW, 1])
        drain(w_unit, ssem.at[G_LOSS, 1])
        drain(lown, ssem.at[G_LOSS, 0])
        drain(gu_sib, sib_s.at[0])
        drain(xs_u.at[pl.ds(0, n_dp - 1)], dp_s.at[0])
        drain(xs_i.at[pl.ds(0, n_dp - 1)], dp_s.at[1])
        drain(normed, ex_s.at[0])
        drain(hidden_all.at[pl.ds(0, 2 * n_dp - 1)], ex_s.at[1])
        drain(dx_all.at[pl.ds(0, 2 * n_dp - 1)], ex_s.at[2])
        drain(dpre_sib, ex_s.at[3])

        def finish(k):
            part_of = rsf.at[0, pl.ds(0, n_z - 1)]
            drain(part_of, ssem.at[G_FRS, k])
            drain(part_of, ssem.at[G_FINZ, k])

            drain(part_of, ssem.at[G_NRS, k])

            @pl.when(s != hub)
            def _():
                drain(ysend.at[k], ssem.at[G_NY, k])

            @pl.when(s == hub)
            def _():
                drain(rsf.at[0], ssem.at[G_NAG, k])

            @pl.when(s < last)
            def _():
                drain(rsf.at[0], ssem.at[G_FAG, k])

            @pl.when(s == last)
            def _():
                drain(osh.at[pl.ds(0, n_seg - 1)], ssem.at[G_FINY, k])

            @pl.when(s > 0)
            def _():
                drain(part_of, ssem.at[G_BRS, k])
                drain(rsf.at[0], ssem.at[G_BAG, k])

        def finish_micro(k):
            drain(stb.at[k, pl.ds(0, n_peer - 1)], ssem.at[G_STAT, k])

        over(chunks, finish)
        over(micros, finish_micro)

    vm = pltpu.VMEM
    lines = (n_z, all_rows, col)
    shard = (chunks, cut, col)
    scatter = (chunks, n_z, cut, col)
    scratch = [
        vm((width, hid_dev), BF16), vm((hid_dev, width), BF16), vm((voc_dev, width), BF16),
        vm(lines, BF16), vm(lines, BF16), vm(lines, BF16),
        vm(scatter, BF16), vm(shard, BF16), vm((2, all_rows, hid_dev), BF16), vm((2, all_rows, hid_dev), F32),
        vm(lines, BF16), vm((all_rows, width), BF16),
        vm((micros, 2, voc_dev, rows), F32), vm((micros, 2, voc_dev, rows), F32),
        vm((micros, n_peer, 4, rows), F32), vm((2, micros, voc_dev, rows), BF16),
        vm(lines, BF16), vm(scatter, BF16), vm(shard, BF16),
        vm((chunks, n_seg - 1, cut, col), BF16), vm(lines, BF16), vm(shard, BF16),
        vm((2, all_rows, hid_dev), BF16), vm(lines, BF16), vm(scatter, BF16), vm(shard, BF16),
        vm(lines, BF16), vm((2 * n_dp, all_rows, hid_dev), BF16),
        vm((2 * n_dp, n_z // n_dp, all_rows, col), BF16), vm((all_rows, hid_dev), BF16),
        vm((n_dp, voc_dev, quarter), F32), vm((n_dp, voc_dev, quarter), BF16), vm((n_dp, voc_dev, quarter), BF16),
        vm((quarter, hid_dev), F32),
        vm((n_dp, voc_dev, quarter), BF16), vm((n_dp, voc_dev, quarter), BF16),
        vm((n_dp, quarter, hid_dev), BF16), vm((n_dp, quarter, hid_dev), BF16),
        vm((8, rows), F32), vm((8, 128), F32), vm((8, 128), F32),
        pltpu.SemaphoreType.DMA((N_GROUPS, chunks)), pltpu.SemaphoreType.DMA((N_GROUPS, chunks)),
        pltpu.SemaphoreType.DMA((1,)), pltpu.SemaphoreType.DMA((1,)),
        pltpu.SemaphoreType.DMA((2,)), pltpu.SemaphoreType.DMA((2,)),
        pltpu.SemaphoreType.DMA((4,)), pltpu.SemaphoreType.DMA((4,)),
    ]
    return kernel, scratch


def solution(mesh):
    n_seg, n_mp, n_dp = mesh.shape["segment"], mesh.shape["mp"], mesh.shape["dp"]

    def on_device(text_rows, durations, unit_targets, w_in, w_out, w_unit):
        micro, rows, width = text_rows.shape
        units = unit_targets.shape[1]
        hid_dev = w_in.shape[2]
        voc_dev = w_unit.shape[1]
        denom = float(micro * units * n_dp)
        kernel, scratch = make_kernel(
            n_seg, n_mp // 2, n_dp, micro // 2, 8, rows, width, hid_dev, voc_dev, units, denom
        )
        quarter = width // n_dp
        vmem = pl.BlockSpec(memory_space=pltpu.VMEM)
        loss, gin, gout, gun = pl.pallas_call(
            kernel,
            out_shape=(
                jax.ShapeDtypeStruct((1,), F32),
                jax.ShapeDtypeStruct((quarter, hid_dev), F32),
                jax.ShapeDtypeStruct((hid_dev, quarter), F32),
                jax.ShapeDtypeStruct((voc_dev, quarter), F32),
            ),
            in_specs=[pl.BlockSpec(memory_space=pl.ANY)] + [vmem] * 5,
            out_specs=(pl.BlockSpec(memory_space=pltpu.SMEM), vmem, vmem, vmem),
            scratch_shapes=scratch,
            compiler_params=pltpu.CompilerParams(
                collective_id=0, has_side_effects=True, vmem_limit_bytes=60 * 1024 * 1024
            ),
        )(
            text_rows, durations, unit_targets, w_in[0], w_out[0],
            jnp.transpose(w_unit),
        )
        return (loss, gin[None], gout[None], jnp.transpose(gun))

    placed = (
        P(None, "dp", None),
        P(None, "dp", None),
        P(None, "dp"),
        P("segment", None, "mp"),
        P("segment", "mp", None),
        P(None, ("segment", "mp")),
    )
    return jax.shard_map(
        on_device,
        mesh=mesh,
        in_specs=placed,
        out_specs=(
            P("dp"),
            P("segment", "dp", "mp"),
            P("segment", "mp", "dp"),
            P("dp", ("segment", "mp")),
        ),
        check_vma=False,
    )
```

```python
import jax
import jax.numpy as jnp
from jax import lax
from jax.experimental import pallas as pl
from jax.experimental.pallas import tpu as pltpu
from jax.sharding import PartitionSpec as P

MESH = pl.DeviceIdType.MESH
F32 = jnp.float32
BF16 = jnp.bfloat16

(
    G_FRS, G_FAG, G_FINY, G_FINZ, G_STAT, G_NRS, G_NY, G_NAG, G_BRS, G_BAG, G_TEXT, G_LOSS, G_SIBW,
) = range(13)
N_GROUPS = 13


def gelu_parts(pre_vals):
    coeff = 0.7978845608
    inner = coeff * (pre_vals + 0.044715 * pre_vals * pre_vals * pre_vals)
    tanh_val = jnp.tanh(inner)
    value = 0.5 * pre_vals * (1.0 + tanh_val)
    slope = 0.5 * (1.0 + tanh_val) + 0.5 * pre_vals * (1.0 - tanh_val * tanh_val) * coeff * (
        1.0 + 3.0 * 0.044715 * pre_vals * pre_vals
    )
    return (value, slope)


def row_scale(floats):
    return lax.rsqrt(jnp.mean(floats * floats, axis=-1, keepdims=True) + 1e-06)


def norm_back(floats, grads):
    scale = row_scale(floats)
    normal = floats * scale
    return scale * (grads - normal * jnp.mean(grads * normal, axis=-1, keepdims=True))


def nn(a, b):
    return jnp.dot(a, b, preferred_element_type=F32)


def nt(a, b):
    return lax.dot_general(a, b, (((1,), (1,)), ((), ())), preferred_element_type=F32)


def tn(a, b):
    return lax.dot_general(a, b, (((0,), (0,)), ((), ())), preferred_element_type=F32)


def make_kernel(n_seg, n_z, n_dp, micros, chunks, rows, width, hid_dev, voc_dev, units, denom):
    all_rows = micros * rows
    cut = all_rows // chunks
    per = chunks // micros
    col = width // n_z
    n_peer = n_seg * n_z
    quarter = width // n_dp
    blocks = n_z // n_dp

    def kernel(
        text, dur, tgt, w_in_h, w_out_h, w_unit_h,
        loss_o, gin_o, gout_o, gun_o,
        w_in, w_out, w_unit, wi_sib, wo_sib, wu_sib,
        xbuf, normed, part, rsf, osh, hid, slo,
        fin, fn, lg, cnt, stb, dlb, partd, rsd, ysend, yrecv, dxb, dsh,
        dpre, partb, rsb, bsh,
        normed_sib, hidden_all, dx_all, dpre_sib, gu_f, gu_sib, gur_sib, gi_f,
        xs_u, xr_u, xs_i, xr_i,
        lvec, lown, lrcv,
        ssem, rsem, sib_s, sib_r, dp_s, dp_r, ex_s, ex_r,
    ):
        s = lax.axis_index("segment")
        mp = lax.axis_index("mp")
        d = lax.axis_index("dp")
        z = lax.div(mp, 2)
        c = lax.rem(mp, 2)
        sib = 2 * z + (1 - c)
        me = s * n_z + z
        last = n_seg - 1
        hub = 0

        def cds(k):
            return pl.ds(pl.multiple_of(k * cut, cut), cut)

        def mds(m):
            return pl.ds(pl.multiple_of(m * rows, rows), rows)

        def whole(buf, where):
            return jnp.concatenate([buf[i, where, :] for i in range(n_z)], axis=-1)

        def columns(i):
            return slice(i * col, (i + 1) * col)

        def put(src, dst, a, b, where):
            pltpu.make_async_remote_copy(
                src_ref=src, dst_ref=dst, send_sem=a, recv_sem=b, device_id=where, device_id_type=MESH
            ).start()

        def drain(ref, sem):
            pltpu.make_async_copy(ref, ref, sem).wait()

        def span(start, stop, fn_of):
            def step(i, carry):
                fn_of(i)
                return carry

            lax.fori_loop(start, stop, step, 0)

        def over(n, fn_of):
            span(0, n, fn_of)

        def peers_z(fn_of):
            def step(i):
                side = 1 - 2 * lax.rem(i, 2)
                off = n_z // 2 + side * lax.div(i + 1, 2)
                fn_of(lax.rem(z + off, n_z))

            over(n_z - 1, step)

        barrier = pltpu.get_barrier_semaphore()

        def greet(where):
            pl.semaphore_signal(barrier, inc=1, device_id=where, device_id_type=MESH)

        peers_z(lambda z2: greet({"mp": 2 * z2 + c}))
        over(n_seg - 1, lambda i: greet({"segment": lax.rem(s + i + 1, n_seg)}))
        over(n_dp - 1, lambda i: greet({"dp": lax.rem(d + i + 1, n_dp)}))
        greet({"mp": sib})

        @pl.when(s == 0)
        def _():
            def load(k):
                for i in range(n_z):
                    pltpu.make_async_copy(
                        text.at[
                            micros * c + lax.div(k, per),
                            pl.ds(pl.multiple_of(lax.rem(k, per) * cut, cut), cut),
                            pl.ds(i * col, col),
                        ],
                        xbuf.at[i, cds(k)],
                        rsem.at[G_TEXT, k],
                    ).start()

            over(chunks, load)

        pltpu.make_async_copy(w_in_h, w_in, rsem.at[G_SIBW, 2]).start()
        pltpu.make_async_copy(w_out_h, w_out, rsem.at[G_SIBW, 3]).start()
        pltpu.make_async_copy(w_unit_h, w_unit, rsem.at[G_LOSS, 2]).start()

        def count(k):
            lengths = dur[micros * c + k].astype(F32)
            lane = lax.broadcasted_iota(jnp.int32, (rows, rows), 1)
            sub = lax.broadcasted_iota(jnp.int32, (rows, rows), 0)
            tri = jnp.where(sub <= lane, 1.0, 0.0).astype(BF16)
            wide = jnp.broadcast_to(lengths, (8, rows)).astype(BF16)
            ends = nn(wide, tri)[0:1, :]
            starts = ends - lengths
            unit = lax.broadcasted_iota(jnp.int32, (units, rows), 0).astype(F32)
            onehot = jnp.where((starts <= unit) & (unit < ends), 1.0, 0.0).astype(BF16)
            target = tgt[pl.ds(micros * c + k, 1), :]
            ids = lax.broadcasted_iota(jnp.int32, (voc_dev, units), 0)
            for h, owner in ((0, mp), (1, sib)):
                first = (s * (2 * n_z) + owner) * voc_dev
                hits = jnp.where(ids + first == target, 1.0, 0.0).astype(BF16)
                cnt[k, h] = nn(hits, onehot)

        over(micros, count)
        pl.semaphore_wait(barrier, n_z - 1 + n_seg - 1 + n_dp - 1 + 1)

        put(w_in_h, wi_sib, ssem.at[G_SIBW, 0], rsem.at[G_SIBW, 0], {"mp": sib})
        put(w_out_h, wo_sib, ssem.at[G_SIBW, 1], rsem.at[G_SIBW, 1], {"mp": sib})
        put(w_unit_h, wu_sib, ssem.at[G_LOSS, 1], rsem.at[G_LOSS, 1], {"mp": sib})

        def scatter_z(buf, got, where, slot, group, k):
            own = got.at[slot, z]
            got[slot, z] = buf[z, where, :]
            peers_z(
                lambda z2: put(
                    buf.at[z2, where], own, ssem.at[group, k], rsem.at[group, k], {"mp": 2 * z2 + c}
                )
            )

        def in_plane(src, dst, group, k):
            peers_z(
                lambda z2: put(src, dst, ssem.at[group, k], rsem.at[group, k], {"mp": 2 * z2 + c})
            )

        def owned_sum(buf, k):
            total = buf[k, 0].astype(F32)
            for i in range(1, n_z):
                total = total + buf[k, i].astype(F32)
            return total

        def forward(k):
            @pl.when(s == 0)
            def _():
                drain(xbuf.at[:, cds(k)], rsem.at[G_TEXT, k])

            @pl.when(s > 0)
            def _():
                drain(xbuf.at[:, cds(k)], rsem.at[G_FAG, k])

            x = whole(xbuf, cds(k)).astype(F32)
            n = (x * row_scale(x)).astype(BF16)
            for i in range(n_z):
                normed[i, cds(k), :] = n[:, columns(i)]

            @pl.when(k == 0)
            def _():
                drain(w_in, rsem.at[G_SIBW, 2])
                drain(w_out, rsem.at[G_SIBW, 3])

            value, slope = gelu_parts(nn(n, w_in[...]))
            h0 = value.astype(BF16)
            hid[0, cds(k), :] = h0
            slo[0, cds(k), :] = slope
            acc = nn(h0, w_out[...])

            @pl.when(k == 0)
            def _():
                drain(wi_sib, rsem.at[G_SIBW, 0])

            value, slope = gelu_parts(nn(n, wi_sib[...]))
            h1 = value.astype(BF16)
            hid[1, cds(k), :] = h1
            slo[1, cds(k), :] = slope

            @pl.when(k == 0)
            def _():
                drain(wo_sib, rsem.at[G_SIBW, 1])

            acc = (acc + nn(h1, wo_sib[...])).astype(BF16)
            for i in range(n_z):
                part[i, cds(k), :] = acc[:, columns(i)]
            scatter_z(part, rsf, cds(k), k, G_FRS, k)

        def forward_end(k):
            drain(rsf.at[k, pl.ds(0, n_z - 1)], rsem.at[G_FRS, k])
            x = xbuf[z, cds(k), :].astype(F32)
            new = (x + owned_sum(rsf, k)).astype(BF16)
            osh[k] = new

            @pl.when(s < last)
            def _():
                def send(z2):
                    put(
                        osh.at[k], xbuf.at[z, cds(k)], ssem.at[G_FAG, k], rsem.at[G_FAG, k],
                        {"segment": s + 1, "mp": 2 * z2 + c},
                    )

                peers_z(send)
                send(z)

            @pl.when(s == last)
            def _():
                fin[z, cds(k), :] = new

                def send(y2):
                    put(
                        osh.at[k], fin.at[z, cds(k)], ssem.at[G_FINY, k], rsem.at[G_FINY, k],
                        {"segment": y2},
                    )

                over(n_seg - 1, send)
                in_plane(osh.at[k], fin.at[z, cds(k)], G_FINZ, k)

        def staged(first, second, start, stop):
            def step(i):
                @pl.when(i < chunks)
                def _():
                    first(i)

                @pl.when(i > 0)
                def _():
                    second(i - 1)

            span(start, stop, step)


        def relay(k):
            drain(fin.at[z, cds(k)], rsem.at[G_FINY, k])
            in_plane(fin.at[z, cds(k)], fin.at[z, cds(k)], G_FINZ, k)

        def logits(k):
            for j in range(per):
                drain(rsf.at[0, pl.ds(0, n_z - 1)], rsem.at[G_FINZ, k * per + j])
            x = whole(fin, mds(k)).astype(F32)
            n = (x * row_scale(x)).astype(BF16)
            fn[mds(k), :] = n
            a = nt(w_unit[...], n)
            b = nt(wu_sib[...], n)
            lg[k, 0] = a
            lg[k, 1] = b
            peak = jnp.maximum(jnp.max(a, axis=0, keepdims=True), jnp.max(b, axis=0, keepdims=True))
            total = jnp.sum(jnp.exp(a - peak), axis=0, keepdims=True) + jnp.sum(
                jnp.exp(b - peak), axis=0, keepdims=True
            )
            hit = jnp.sum(cnt[k, 0] * a, axis=0, keepdims=True) + jnp.sum(
                cnt[k, 1] * b, axis=0, keepdims=True
            )
            sub = lax.broadcasted_iota(jnp.int32, (4, rows), 0)
            stb[k, me] = jnp.where(sub == 0, peak, jnp.where(sub == 1, total, hit))

            def send(i):
                side = 1 - 2 * lax.rem(i, 2)
                other = lax.rem(me + n_peer // 2 + side * lax.div(i + 1, 2), n_peer)
                put(
                    stb.at[k, me], stb.at[k, me], ssem.at[G_STAT, k], rsem.at[G_STAT, k],
                    {"segment": lax.div(other, n_z), "mp": 2 * lax.rem(other, n_z) + c},
                )

            over(n_peer - 1, send)

        def dlogits(k):
            drain(stb.at[k, pl.ds(0, n_peer - 1)], rsem.at[G_STAT, k])
            every = stb[k]
            peaks = every[:, 0:1, :]
            peak = jnp.max(peaks, axis=0)
            total = jnp.sum(every[:, 1:2, :] * jnp.exp(peaks - peak[None]), axis=0)
            hit = jnp.sum(every[:, 2:3, :], axis=0)
            lse = peak + jnp.log(total)
            lengths = dur[micros * c + k].astype(F32)
            lvec[0:1, :] += lengths * lse - hit
            acc = None
            for h, w in ((0, w_unit), (1, wu_sib)):
                grad = (lengths * jnp.exp(lg[k, h] - lse) - cnt[k, h]) * (1.0 / denom)
                grad = grad.astype(BF16)
                dlb[h, k] = grad
                term = tn(grad, w[...])
                acc = term if acc is None else acc + term
            x = whole(fin, mds(k)).astype(F32)
            acc = norm_back(x, acc).astype(BF16)
            for i in range(n_z):
                partd[i, mds(k), :] = acc[:, columns(i)]
            span(k * per, (k + 1) * per, lambda j: scatter_z(partd, rsd, cds(j), j, G_NRS, j))

        def norm_sum(k):
            drain(rsd.at[k, pl.ds(0, n_z - 1)], rsem.at[G_NRS, k])
            ysend[k] = owned_sum(rsd, k).astype(BF16)

            @pl.when(s != hub)
            def _():
                put(ysend.at[k], yrecv.at[k, s - 1], ssem.at[G_NY, k], rsem.at[G_NY, k], {"segment": hub})

        def norm_end(k):
            drain(yrecv.at[k], rsem.at[G_NY, k])
            total = ysend[k].astype(F32)
            for i in range(n_seg - 1):
                total = total + yrecv[k, i].astype(F32)
            dsh[k] = total.astype(BF16)

            def send(z2):
                put(
                    dsh.at[k], dxb.at[z, cds(k)], ssem.at[G_NAG, k], rsem.at[G_NAG, k],
                    {"segment": last, "mp": 2 * z2 + c},
                )

            peers_z(send)
            send(z)

        def dp_send(xs, xr, g):
            def step(off):
                d2 = lax.rem(d + off + 1, n_dp)
                put(xs.at[d2], xr.at[d], dp_s.at[g], dp_r.at[g], {"dp": d2})

            over(n_dp - 1, step)

        def dp_out(own, xr, g, out):
            drain(xr.at[pl.ds(0, n_dp - 1)], dp_r.at[g])
            total = own
            for off in range(1, n_dp):
                total = total + xr[lax.rem(d + off, n_dp)].astype(F32)
            out[...] = total

        def unit_grad():
            lown[...] = jnp.broadcast_to(jnp.sum(lvec[...], keepdims=True), lown.shape)
            put(lown, lrcv, ssem.at[G_LOSS, 0], rsem.at[G_LOSS, 0], {"mp": sib})
            for h in (1, 0):
                total = nn(dlb[h, 0], fn[pl.ds(0, rows), :])
                for k in range(1, micros):
                    total = total + nn(dlb[h, k], fn[pl.ds(k * rows, rows), :])
                for q in range(n_dp):
                    piece = total[:, q * quarter : (q + 1) * quarter]
                    if h == 1:
                        gu_sib[q] = piece.astype(BF16)
                    else:
                        gu_f[q] = piece
                if h == 1:
                    put(gu_sib, gur_sib, sib_s.at[0], sib_r.at[0], {"mp": sib})
            drain(gur_sib, sib_r.at[0])

            def unit_sum(q):
                total = gu_f[q] + gur_sib[q].astype(F32)
                gu_f[q] = total
                xs_u[q] = total.astype(BF16)

            over(n_dp, unit_sum)
            dp_send(xs_u, xr_u, 0)

        def backward(k):
            @pl.when(s == last)
            def _():
                drain(dxb.at[:, cds(k)], rsem.at[G_NAG, k])

            @pl.when(s < last)
            def _():
                drain(dxb.at[:, cds(k)], rsem.at[G_BAG, k])

            g = whole(dxb, cds(k))
            p0 = (nt(g, w_out[...]) * slo[0, cds(k), :]).astype(BF16)
            dpre[0, cds(k), :] = p0
            p1 = (nt(g, wo_sib[...]) * slo[1, cds(k), :]).astype(BF16)
            dpre[1, cds(k), :] = p1

            @pl.when(s > 0)
            def _():
                x = whole(xbuf, cds(k)).astype(F32)
                acc = norm_back(x, nt(p0, w_in[...]) + nt(p1, wi_sib[...])).astype(BF16)
                for i in range(n_z):
                    partb[i, cds(k), :] = acc[:, columns(i)]
                scatter_z(partb, rsb, cds(k), k, G_BRS, k)

            put(dpre.at[1, cds(k)], dpre_sib.at[cds(k)], ex_s.at[3], ex_r.at[3], {"mp": sib})

            def share(off):
                other = lax.rem(2 * d + c + off, 2 * n_dp)
                d2 = lax.div(other, 2)
                put(
                    dxb.at[pl.ds(d2 * blocks, blocks), cds(k)], dx_all.at[2 * d + c, :, cds(k)],
                    ex_s.at[2], ex_r.at[2], {"dp": d2, "mp": 2 * z + lax.rem(other, 2)},
                )

            span(1, 2 * n_dp, share)

        def backward_end(k):
            @pl.when(s > 0)
            def _():
                drain(rsb.at[k, pl.ds(0, n_z - 1)], rsem.at[G_BRS, k])
                bsh[k] = (dxb[z, cds(k), :].astype(F32) + owned_sum(rsb, k)).astype(BF16)

                def send(z2):
                    put(
                        bsh.at[k], dxb.at[z, cds(k)], ssem.at[G_BAG, k], rsem.at[G_BAG, k],
                        {"segment": s - 1, "mp": 2 * z2 + c},
                    )

                peers_z(send)
                send(z)

        def share_hidden():
            put(normed, normed_sib, ex_s.at[0], ex_r.at[0], {"mp": sib})

            def step(off):
                other = lax.rem(2 * d + c + off, 2 * n_dp)
                c2 = lax.rem(other, 2)
                put(
                    hid.at[lax.rem(c + c2, 2)], hidden_all.at[2 * d + c],
                    ex_s.at[1], ex_r.at[1], {"dp": lax.div(other, 2), "mp": 2 * z + c2},
                )

            span(1, 2 * n_dp, step)

        early = per + 1
        staged(forward, forward_end, 0, early + 1)
        drain(wu_sib, rsem.at[G_LOSS, 1])
        drain(w_unit, rsem.at[G_LOSS, 2])
        lvec[...] = jnp.zeros_like(lvec)

        @pl.when(s == last)
        def _():
            logits(0)

        staged(forward, forward_end, early + 1, chunks + 1)

        @pl.when(s < last)
        def _():
            over(early, relay)
            logits(0)
            span(early, chunks, relay)
            share_hidden()

        dlogits(0)
        logits(1)

        over(per - 1, norm_sum)

        @pl.when(s == hub)
        def _():
            norm_end(0)

        dlogits(1)
        norm_sum(per - 1)

        @pl.when(s == hub)
        def _():
            span(1, per, norm_end)

        @pl.when(s < last)
        def _():
            def late(i):
                @pl.when(i < chunks)
                def _():
                    norm_sum(i)

                @pl.when((s == hub) & (i >= per + 2))
                def _():
                    norm_end(i - 2)

            span(per, chunks + 2, late)
            unit_grad()
            staged(backward, backward_end, 0, chunks + 1)

        @pl.when(s == last)
        def _():
            share_hidden()

            def first_half(i):
                backward(i)
                norm_sum(per + i)

            over(per, first_half)
            over(per, backward_end)
            span(per, chunks, backward)
            span(per, chunks, backward_end)
            unit_grad()

        drain(dpre_sib, ex_r.at[3])
        drain(normed_sib, ex_r.at[0])

        def in_quarter(q):
            own = jnp.concatenate([normed[q * blocks + i] for i in range(blocks)], axis=-1)
            other = jnp.concatenate([normed_sib[q * blocks + i] for i in range(blocks)], axis=-1)
            return tn(own, dpre[0]) + tn(other, dpre_sib[...])

        def in_send(i):
            side = 1 - 2 * lax.rem(i, 2)
            d2 = lax.rem(d + n_dp // 2 + side * lax.div(i + 1, 2), n_dp)
            xs_i[d2] = in_quarter(d2).astype(BF16)
            put(xs_i.at[d2], xr_i.at[d], dp_s.at[1], dp_r.at[1], {"dp": d2})

        over(n_dp - 1, in_send)
        gi_f[...] = in_quarter(d)

        drain(hidden_all.at[pl.ds(0, 2 * n_dp - 1)], ex_r.at[1])
        drain(dx_all.at[pl.ds(0, 2 * n_dp - 1)], ex_r.at[2])
        own_dx = jnp.concatenate([dxb[d * blocks + i] for i in range(blocks)], axis=-1)
        gout_o[...] = tn(hid[0], own_dx)

        def out_term(off):
            other = lax.rem(2 * d + c + off, 2 * n_dp)
            got = jnp.concatenate([dx_all[other, i] for i in range(blocks)], axis=-1)
            gout_o[...] += tn(hidden_all[other], got)

        span(1, 2 * n_dp, out_term)

        dp_out(gu_f[d], xr_u, 0, gun_o)
        drain(lrcv, rsem.at[G_LOSS, 0])
        loss_o[0] = jnp.max(lown[...] + lrcv[...]) * (1.0 / denom)
        dp_out(gi_f[...], xr_i, 1, gin_o)

        drain(w_in, ssem.at[G_SIBW, 0])
        drain(w_out, ssem.at[G_SIBW, 1])
        drain(w_unit, ssem.at[G_LOSS, 1])
        drain(lown, ssem.at[G_LOSS, 0])
        drain(gu_sib, sib_s.at[0])
        drain(xs_u.at[pl.ds(0, n_dp - 1)], dp_s.at[0])
        drain(xs_i.at[pl.ds(0, n_dp - 1)], dp_s.at[1])
        drain(normed, ex_s.at[0])
        drain(hidden_all.at[pl.ds(0, 2 * n_dp - 1)], ex_s.at[1])
        drain(dx_all.at[pl.ds(0, 2 * n_dp - 1)], ex_s.at[2])
        drain(dpre_sib, ex_s.at[3])

        def finish(k):
            part_of = rsf.at[0, pl.ds(0, n_z - 1)]
            drain(part_of, ssem.at[G_FRS, k])
            drain(part_of, ssem.at[G_FINZ, k])

            drain(part_of, ssem.at[G_NRS, k])

            @pl.when(s != hub)
            def _():
                drain(ysend.at[k], ssem.at[G_NY, k])

            @pl.when(s == hub)
            def _():
                drain(rsf.at[0], ssem.at[G_NAG, k])

            @pl.when(s < last)
            def _():
                drain(rsf.at[0], ssem.at[G_FAG, k])

            @pl.when(s == last)
            def _():
                drain(osh.at[pl.ds(0, n_seg - 1)], ssem.at[G_FINY, k])

            @pl.when(s > 0)
            def _():
                drain(part_of, ssem.at[G_BRS, k])
                drain(rsf.at[0], ssem.at[G_BAG, k])

        def finish_micro(k):
            drain(stb.at[k, pl.ds(0, n_peer - 1)], ssem.at[G_STAT, k])

        over(chunks, finish)
        over(micros, finish_micro)

    vm = pltpu.VMEM
    lines = (n_z, all_rows, col)
    shard = (chunks, cut, col)
    scatter = (chunks, n_z, cut, col)
    scratch = [
        vm((width, hid_dev), BF16), vm((hid_dev, width), BF16), vm((voc_dev, width), BF16),
        vm((width, hid_dev), BF16), vm((hid_dev, width), BF16), vm((voc_dev, width), BF16),
        vm(lines, BF16), vm(lines, BF16), vm(lines, BF16),
        vm(scatter, BF16), vm(shard, BF16), vm((2, all_rows, hid_dev), BF16), vm((2, all_rows, hid_dev), F32),
        vm(lines, BF16), vm((all_rows, width), BF16),
        vm((micros, 2, voc_dev, rows), F32), vm((micros, 2, voc_dev, rows), F32),
        vm((micros, n_peer, 4, rows), F32), vm((2, micros, voc_dev, rows), BF16),
        vm(lines, BF16), vm(scatter, BF16), vm(shard, BF16),
        vm((chunks, n_seg - 1, cut, col), BF16), vm(lines, BF16), vm(shard, BF16),
        vm((2, all_rows, hid_dev), BF16), vm(lines, BF16), vm(scatter, BF16), vm(shard, BF16),
        vm(lines, BF16), vm((2 * n_dp, all_rows, hid_dev), BF16),
        vm((2 * n_dp, n_z // n_dp, all_rows, col), BF16), vm((all_rows, hid_dev), BF16),
        vm((n_dp, voc_dev, quarter), F32), vm((n_dp, voc_dev, quarter), BF16), vm((n_dp, voc_dev, quarter), BF16),
        vm((quarter, hid_dev), F32),
        vm((n_dp, voc_dev, quarter), BF16), vm((n_dp, voc_dev, quarter), BF16),
        vm((n_dp, quarter, hid_dev), BF16), vm((n_dp, quarter, hid_dev), BF16),
        vm((8, rows), F32), vm((8, 128), F32), vm((8, 128), F32),
        pltpu.SemaphoreType.DMA((N_GROUPS, chunks)), pltpu.SemaphoreType.DMA((N_GROUPS, chunks)),
        pltpu.SemaphoreType.DMA((1,)), pltpu.SemaphoreType.DMA((1,)),
        pltpu.SemaphoreType.DMA((2,)), pltpu.SemaphoreType.DMA((2,)),
        pltpu.SemaphoreType.DMA((4,)), pltpu.SemaphoreType.DMA((4,)),
    ]
    return kernel, scratch


def solution(mesh):
    n_seg, n_mp, n_dp = mesh.shape["segment"], mesh.shape["mp"], mesh.shape["dp"]

    def on_device(text_rows, durations, unit_targets, w_in, w_out, w_unit):
        micro, rows, width = text_rows.shape
        units = unit_targets.shape[1]
        hid_dev = w_in.shape[2]
        voc_dev = w_unit.shape[1]
        denom = float(micro * units * n_dp)
        kernel, scratch = make_kernel(
            n_seg, n_mp // 2, n_dp, micro // 2, 8, rows, width, hid_dev, voc_dev, units, denom
        )
        quarter = width // n_dp
        vmem = pl.BlockSpec(memory_space=pltpu.VMEM)
        hbm = pl.BlockSpec(memory_space=pl.ANY)
        loss, gin, gout, gun = pl.pallas_call(
            kernel,
            out_shape=(
                jax.ShapeDtypeStruct((1,), F32),
                jax.ShapeDtypeStruct((quarter, hid_dev), F32),
                jax.ShapeDtypeStruct((hid_dev, quarter), F32),
                jax.ShapeDtypeStruct((voc_dev, quarter), F32),
            ),
            in_specs=[hbm, vmem, vmem, hbm, hbm, hbm],
            out_specs=(pl.BlockSpec(memory_space=pltpu.SMEM), vmem, vmem, vmem),
            scratch_shapes=scratch,
            compiler_params=pltpu.CompilerParams(
                collective_id=0, has_side_effects=True, vmem_limit_bytes=60 * 1024 * 1024
            ),
        )(
            text_rows, durations, unit_targets, w_in[0], w_out[0],
            jnp.transpose(w_unit),
        )
        return (loss, gin[None], gout[None], jnp.transpose(gun))

    placed = (
        P(None, "dp", None),
        P(None, "dp", None),
        P(None, "dp"),
        P("segment", None, "mp"),
        P("segment", "mp", None),
        P(None, ("segment", "mp")),
    )
    return jax.shard_map(
        on_device,
        mesh=mesh,
        in_specs=placed,
        out_specs=(
            P("dp"),
            P("segment", "dp", "mp"),
            P("segment", "mp", "dp"),
            P("dp", ("segment", "mp")),
        ),
        check_vma=False,
    )
```

```python
import jax
import jax.numpy as jnp
from jax import lax
from jax.experimental import pallas as pl
from jax.experimental.pallas import tpu as pltpu
from jax.sharding import PartitionSpec as P

MESH = pl.DeviceIdType.MESH
F32 = jnp.float32
BF16 = jnp.bfloat16

(
    G_FRS, G_FAG, G_FINY, G_FINZ, G_STAT, G_NRS, G_NY, G_NAG, G_BRS, G_BAG, G_TEXT, G_LOSS, G_SIBW,
) = range(13)
N_GROUPS = 13


def gelu_parts(pre_vals):
    coeff = 0.7978845608
    inner = coeff * (pre_vals + 0.044715 * pre_vals * pre_vals * pre_vals)
    tanh_val = jnp.tanh(inner)
    value = 0.5 * pre_vals * (1.0 + tanh_val)
    slope = 0.5 * (1.0 + tanh_val) + 0.5 * pre_vals * (1.0 - tanh_val * tanh_val) * coeff * (
        1.0 + 3.0 * 0.044715 * pre_vals * pre_vals
    )
    return (value, slope)


def row_scale(floats):
    return lax.rsqrt(jnp.mean(floats * floats, axis=-1, keepdims=True) + 1e-06)


def norm_back(floats, grads):
    scale = row_scale(floats)
    normal = floats * scale
    return scale * (grads - normal * jnp.mean(grads * normal, axis=-1, keepdims=True))


def nn(a, b):
    return jnp.dot(a, b, preferred_element_type=F32)


def nt(a, b):
    return lax.dot_general(a, b, (((1,), (1,)), ((), ())), preferred_element_type=F32)


def tn(a, b):
    return lax.dot_general(a, b, (((0,), (0,)), ((), ())), preferred_element_type=F32)


def make_kernel(n_seg, n_z, n_dp, micros, chunks, rows, width, hid_dev, voc_dev, units, denom):
    all_rows = micros * rows
    cut = all_rows // chunks
    per = chunks // micros
    col = width // n_z
    n_peer = n_seg * n_z
    quarter = width // n_dp
    blocks = n_z // n_dp

    def kernel(
        text, dur, tgt, w_in_h, w_out_h, w_unit_h,
        loss_o, gin_o, gi_f, gout_o, gun_o,
        w_in, w_out, w_unit, wi_sib, wo_sib, wu_sib,
        xbuf, normed, part, rsf, osh, hid, slo,
        fin, fn, lg, cnt, stb, dlb, partd, rsd, ysend, yrecv, dxb, dsh,
        dpre, partb, rsb, bsh,
        normed_sib, hidden_all, dx_all, dpre_sib, gu_f, gu_sib, gur_sib,
        xs_u, xr_u, xs_i, xr_i,
        lvec, lown, lrcv,
        ssem, rsem, sib_s, sib_r, dp_s, dp_r, ex_s, ex_r,
    ):
        s = lax.axis_index("segment")
        mp = lax.axis_index("mp")
        d = lax.axis_index("dp")
        z = lax.div(mp, 2)
        c = lax.rem(mp, 2)
        sib = 2 * z + (1 - c)
        me = s * n_z + z
        last = n_seg - 1
        hub = 0

        def cds(k):
            return pl.ds(pl.multiple_of(k * cut, cut), cut)

        def mds(m):
            return pl.ds(pl.multiple_of(m * rows, rows), rows)

        def whole(buf, where):
            return jnp.concatenate([buf[i, where, :] for i in range(n_z)], axis=-1)

        def columns(i):
            return slice(i * col, (i + 1) * col)

        def put(src, dst, a, b, where):
            pltpu.make_async_remote_copy(
                src_ref=src, dst_ref=dst, send_sem=a, recv_sem=b, device_id=where, device_id_type=MESH
            ).start()

        def drain(ref, sem):
            pltpu.make_async_copy(ref, ref, sem).wait()

        def span(start, stop, fn_of):
            def step(i, carry):
                fn_of(i)
                return carry

            lax.fori_loop(start, stop, step, 0)

        def over(n, fn_of):
            span(0, n, fn_of)

        def peers_z(fn_of):
            def step(i):
                side = 1 - 2 * lax.rem(i, 2)
                off = n_z // 2 + side * lax.div(i + 1, 2)
                fn_of(lax.rem(z + off, n_z))

            over(n_z - 1, step)

        barrier = pltpu.get_barrier_semaphore()

        def greet(where):
            pl.semaphore_signal(barrier, inc=1, device_id=where, device_id_type=MESH)

        peers_z(lambda z2: greet({"mp": 2 * z2 + c}))
        over(n_seg - 1, lambda i: greet({"segment": lax.rem(s + i + 1, n_seg)}))
        over(n_dp - 1, lambda i: greet({"dp": lax.rem(d + i + 1, n_dp)}))
        greet({"mp": sib})

        @pl.when(s == 0)
        def _():
            def load(k):
                for i in range(n_z):
                    pltpu.make_async_copy(
                        text.at[
                            micros * c + lax.div(k, per),
                            pl.ds(pl.multiple_of(lax.rem(k, per) * cut, cut), cut),
                            pl.ds(i * col, col),
                        ],
                        xbuf.at[i, cds(k)],
                        rsem.at[G_TEXT, k],
                    ).start()

            over(chunks, load)

        pltpu.make_async_copy(w_in_h, w_in, rsem.at[G_SIBW, 2]).start()
        pltpu.make_async_copy(w_out_h, w_out, rsem.at[G_SIBW, 3]).start()
        pltpu.make_async_copy(w_unit_h, w_unit, rsem.at[G_LOSS, 2]).start()

        def count(k):
            lengths = dur[micros * c + k].astype(F32)
            lane = lax.broadcasted_iota(jnp.int32, (rows, rows), 1)
            sub = lax.broadcasted_iota(jnp.int32, (rows, rows), 0)
            tri = jnp.where(sub <= lane, 1.0, 0.0).astype(BF16)
            wide = jnp.broadcast_to(lengths, (8, rows)).astype(BF16)
            ends = nn(wide, tri)[0:1, :]
            starts = ends - lengths
            unit = lax.broadcasted_iota(jnp.int32, (units, rows), 0).astype(F32)
            onehot = jnp.where((starts <= unit) & (unit < ends), 1.0, 0.0).astype(BF16)
            target = tgt[pl.ds(micros * c + k, 1), :]
            ids = lax.broadcasted_iota(jnp.int32, (voc_dev, units), 0)
            for h, owner in ((0, mp), (1, sib)):
                first = (s * (2 * n_z) + owner) * voc_dev
                hits = jnp.where(ids + first == target, 1.0, 0.0).astype(BF16)
                cnt[k, h] = nn(hits, onehot)

        over(micros, count)
        pl.semaphore_wait(barrier, n_z - 1 + n_seg - 1 + n_dp - 1 + 1)

        put(w_in_h, wi_sib, ssem.at[G_SIBW, 0], rsem.at[G_SIBW, 0], {"mp": sib})
        put(w_out_h, wo_sib, ssem.at[G_SIBW, 1], rsem.at[G_SIBW, 1], {"mp": sib})
        put(w_unit_h, wu_sib, ssem.at[G_LOSS, 1], rsem.at[G_LOSS, 1], {"mp": sib})

        def scatter_z(buf, got, where, slot, group, k):
            own = got.at[slot, z]
            got[slot, z] = buf[z, where, :]
            peers_z(
                lambda z2: put(
                    buf.at[z2, where], own, ssem.at[group, k], rsem.at[group, k], {"mp": 2 * z2 + c}
                )
            )

        def in_plane(src, dst, group, k):
            peers_z(
                lambda z2: put(src, dst, ssem.at[group, k], rsem.at[group, k], {"mp": 2 * z2 + c})
            )

        def owned_sum(buf, k):
            total = buf[k, 0].astype(F32)
            for i in range(1, n_z):
                total = total + buf[k, i].astype(F32)
            return total

        def forward(k):
            @pl.when(s == 0)
            def _():
                drain(xbuf.at[:, cds(k)], rsem.at[G_TEXT, k])

            @pl.when(s > 0)
            def _():
                drain(xbuf.at[:, cds(k)], rsem.at[G_FAG, k])

            x = whole(xbuf, cds(k)).astype(F32)
            n = (x * row_scale(x)).astype(BF16)
            for i in range(n_z):
                normed[i, cds(k), :] = n[:, columns(i)]

            @pl.when(k == 0)
            def _():
                drain(w_in, rsem.at[G_SIBW, 2])
                drain(w_out, rsem.at[G_SIBW, 3])

            value, slope = gelu_parts(nn(n, w_in[...]))
            h0 = value.astype(BF16)
            hid[0, cds(k), :] = h0
            slo[0, cds(k), :] = slope
            acc = nn(h0, w_out[...])

            @pl.when(k == 0)
            def _():
                drain(wi_sib, rsem.at[G_SIBW, 0])

            value, slope = gelu_parts(nn(n, wi_sib[...]))
            h1 = value.astype(BF16)
            hid[1, cds(k), :] = h1
            slo[1, cds(k), :] = slope

            @pl.when(k == 0)
            def _():
                drain(wo_sib, rsem.at[G_SIBW, 1])

            acc = (acc + nn(h1, wo_sib[...])).astype(BF16)
            for i in range(n_z):
                part[i, cds(k), :] = acc[:, columns(i)]
            scatter_z(part, rsf, cds(k), k, G_FRS, k)

        def forward_end(k):
            drain(rsf.at[k, pl.ds(0, n_z - 1)], rsem.at[G_FRS, k])
            x = xbuf[z, cds(k), :].astype(F32)
            new = (x + owned_sum(rsf, k)).astype(BF16)
            osh[k] = new

            @pl.when(s < last)
            def _():
                def send(z2):
                    put(
                        osh.at[k], xbuf.at[z, cds(k)], ssem.at[G_FAG, k], rsem.at[G_FAG, k],
                        {"segment": s + 1, "mp": 2 * z2 + c},
                    )

                peers_z(send)
                send(z)

            @pl.when(s == last)
            def _():
                fin[z, cds(k), :] = new

                def send(y2):
                    put(
                        osh.at[k], fin.at[z, cds(k)], ssem.at[G_FINY, k], rsem.at[G_FINY, k],
                        {"segment": y2},
                    )

                over(n_seg - 1, send)
                in_plane(osh.at[k], fin.at[z, cds(k)], G_FINZ, k)

        def staged(first, second, start, stop):
            def step(i):
                @pl.when(i < chunks)
                def _():
                    first(i)

                @pl.when(i > 0)
                def _():
                    second(i - 1)

            span(start, stop, step)


        def relay(k):
            drain(fin.at[z, cds(k)], rsem.at[G_FINY, k])
            in_plane(fin.at[z, cds(k)], fin.at[z, cds(k)], G_FINZ, k)

        def logits(k):
            for j in range(per):
                drain(rsf.at[0, pl.ds(0, n_z - 1)], rsem.at[G_FINZ, k * per + j])
            x = whole(fin, mds(k)).astype(F32)
            n = (x * row_scale(x)).astype(BF16)
            fn[mds(k), :] = n
            a = nt(w_unit[...], n)
            b = nt(wu_sib[...], n)
            lg[k, 0] = a
            lg[k, 1] = b
            peak = jnp.maximum(jnp.max(a, axis=0, keepdims=True), jnp.max(b, axis=0, keepdims=True))
            total = jnp.sum(jnp.exp(a - peak), axis=0, keepdims=True) + jnp.sum(
                jnp.exp(b - peak), axis=0, keepdims=True
            )
            hit = jnp.sum(cnt[k, 0] * a, axis=0, keepdims=True) + jnp.sum(
                cnt[k, 1] * b, axis=0, keepdims=True
            )
            sub = lax.broadcasted_iota(jnp.int32, (4, rows), 0)
            stb[k, me] = jnp.where(sub == 0, peak, jnp.where(sub == 1, total, hit))

            def send(i):
                side = 1 - 2 * lax.rem(i, 2)
                other = lax.rem(me + n_peer // 2 + side * lax.div(i + 1, 2), n_peer)
                put(
                    stb.at[k, me], stb.at[k, me], ssem.at[G_STAT, k], rsem.at[G_STAT, k],
                    {"segment": lax.div(other, n_z), "mp": 2 * lax.rem(other, n_z) + c},
                )

            over(n_peer - 1, send)

        def dlogits(k):
            drain(stb.at[k, pl.ds(0, n_peer - 1)], rsem.at[G_STAT, k])
            every = stb[k]
            peaks = every[:, 0:1, :]
            peak = jnp.max(peaks, axis=0)
            total = jnp.sum(every[:, 1:2, :] * jnp.exp(peaks - peak[None]), axis=0)
            hit = jnp.sum(every[:, 2:3, :], axis=0)
            lse = peak + jnp.log(total)
            lengths = dur[micros * c + k].astype(F32)
            lvec[0:1, :] += lengths * lse - hit
            acc = None
            for h, w in ((0, w_unit), (1, wu_sib)):
                grad = (lengths * jnp.exp(lg[k, h] - lse) - cnt[k, h]) * (1.0 / denom)
                grad = grad.astype(BF16)
                dlb[h, k] = grad
                term = tn(grad, w[...])
                acc = term if acc is None else acc + term
            x = whole(fin, mds(k)).astype(F32)
            acc = norm_back(x, acc).astype(BF16)
            for i in range(n_z):
                partd[i, mds(k), :] = acc[:, columns(i)]
            span(k * per, (k + 1) * per, lambda j: scatter_z(partd, rsd, cds(j), j, G_NRS, j))

        def norm_sum(k):
            drain(rsd.at[k, pl.ds(0, n_z - 1)], rsem.at[G_NRS, k])
            ysend[k] = owned_sum(rsd, k).astype(BF16)

            @pl.when(s != hub)
            def _():
                put(ysend.at[k], yrecv.at[k, s - 1], ssem.at[G_NY, k], rsem.at[G_NY, k], {"segment": hub})

        def norm_end(k):
            drain(yrecv.at[k], rsem.at[G_NY, k])
            total = ysend[k].astype(F32)
            for i in range(n_seg - 1):
                total = total + yrecv[k, i].astype(F32)
            dsh[k] = total.astype(BF16)

            def send(z2):
                put(
                    dsh.at[k], dxb.at[z, cds(k)], ssem.at[G_NAG, k], rsem.at[G_NAG, k],
                    {"segment": last, "mp": 2 * z2 + c},
                )

            peers_z(send)
            send(z)

        def dp_send(xs, xr, g):
            def step(off):
                d2 = lax.rem(d + off + 1, n_dp)
                put(xs.at[d2], xr.at[d], dp_s.at[g], dp_r.at[g], {"dp": d2})

            over(n_dp - 1, step)

        def dp_out(own, xr, g, out):
            drain(xr.at[pl.ds(0, n_dp - 1)], dp_r.at[g])
            total = own
            for off in range(1, n_dp):
                term = xr[lax.rem(d + off, n_dp)].astype(F32)
                total = term if total is None else total + term
            out[...] = total

        def unit_grad():
            lown[...] = jnp.broadcast_to(jnp.sum(lvec[...], keepdims=True), lown.shape)
            put(lown, lrcv, ssem.at[G_LOSS, 0], rsem.at[G_LOSS, 0], {"mp": sib})
            for h in (1, 0):
                total = nn(dlb[h, 0], fn[pl.ds(0, rows), :])
                for k in range(1, micros):
                    total = total + nn(dlb[h, k], fn[pl.ds(k * rows, rows), :])
                for q in range(n_dp):
                    piece = total[:, q * quarter : (q + 1) * quarter]
                    if h == 1:
                        gu_sib[q] = piece.astype(BF16)
                    else:
                        gu_f[q] = piece
                if h == 1:
                    put(gu_sib, gur_sib, sib_s.at[0], sib_r.at[0], {"mp": sib})
            drain(gur_sib, sib_r.at[0])

            def unit_sum(q):
                total = gu_f[q] + gur_sib[q].astype(F32)
                gu_f[q] = total
                xs_u[q] = total.astype(BF16)

            over(n_dp, unit_sum)
            dp_send(xs_u, xr_u, 0)

        def backward(k):
            @pl.when(s == last)
            def _():
                drain(dxb.at[:, cds(k)], rsem.at[G_NAG, k])

            @pl.when(s < last)
            def _():
                drain(dxb.at[:, cds(k)], rsem.at[G_BAG, k])

            g = whole(dxb, cds(k))
            p0 = (nt(g, w_out[...]) * slo[0, cds(k), :]).astype(BF16)
            dpre[0, cds(k), :] = p0
            p1 = (nt(g, wo_sib[...]) * slo[1, cds(k), :]).astype(BF16)
            dpre[1, cds(k), :] = p1

            @pl.when(s > 0)
            def _():
                x = whole(xbuf, cds(k)).astype(F32)
                acc = norm_back(x, nt(p0, w_in[...]) + nt(p1, wi_sib[...])).astype(BF16)
                for i in range(n_z):
                    partb[i, cds(k), :] = acc[:, columns(i)]
                scatter_z(partb, rsb, cds(k), k, G_BRS, k)

            put(dpre.at[1, cds(k)], dpre_sib.at[cds(k)], ex_s.at[3], ex_r.at[3], {"mp": sib})

            def share(off):
                other = lax.rem(2 * d + c + off, 2 * n_dp)
                d2 = lax.div(other, 2)
                put(
                    dxb.at[pl.ds(d2 * blocks, blocks), cds(k)], dx_all.at[2 * d + c, :, cds(k)],
                    ex_s.at[2], ex_r.at[2], {"dp": d2, "mp": 2 * z + lax.rem(other, 2)},
                )

            span(1, 2 * n_dp, share)

        def backward_end(k):
            @pl.when(s > 0)
            def _():
                drain(rsb.at[k, pl.ds(0, n_z - 1)], rsem.at[G_BRS, k])
                bsh[k] = (dxb[z, cds(k), :].astype(F32) + owned_sum(rsb, k)).astype(BF16)

                def send(z2):
                    put(
                        bsh.at[k], dxb.at[z, cds(k)], ssem.at[G_BAG, k], rsem.at[G_BAG, k],
                        {"segment": s - 1, "mp": 2 * z2 + c},
                    )

                peers_z(send)
                send(z)

        def share_hidden():
            put(normed, normed_sib, ex_s.at[0], ex_r.at[0], {"mp": sib})

            def step(off):
                other = lax.rem(2 * d + c + off, 2 * n_dp)
                c2 = lax.rem(other, 2)
                put(
                    hid.at[lax.rem(c + c2, 2)], hidden_all.at[2 * d + c],
                    ex_s.at[1], ex_r.at[1], {"dp": lax.div(other, 2), "mp": 2 * z + c2},
                )

            span(1, 2 * n_dp, step)

        early = per + 1
        staged(forward, forward_end, 0, early + 1)
        drain(wu_sib, rsem.at[G_LOSS, 1])
        drain(w_unit, rsem.at[G_LOSS, 2])
        lvec[...] = jnp.zeros_like(lvec)

        @pl.when(s == last)
        def _():
            logits(0)

        staged(forward, forward_end, early + 1, chunks + 1)

        @pl.when(s < last)
        def _():
            over(early, relay)
            logits(0)
            span(early, chunks, relay)
            share_hidden()

        dlogits(0)
        logits(1)

        over(per - 1, norm_sum)

        @pl.when(s == hub)
        def _():
            norm_end(0)

        dlogits(1)
        norm_sum(per - 1)

        @pl.when(s == hub)
        def _():
            span(1, per, norm_end)

        @pl.when(s < last)
        def _():
            def late(i):
                @pl.when(i < chunks)
                def _():
                    norm_sum(i)

                @pl.when((s == hub) & (i >= per + 2))
                def _():
                    norm_end(i - 2)

            span(per, chunks + 2, late)
            unit_grad()
            staged(backward, backward_end, 0, chunks + 1)

        @pl.when(s == last)
        def _():
            share_hidden()

            def first_half(i):
                backward(i)
                norm_sum(per + i)

            over(per, first_half)
            over(per, backward_end)
            span(per, chunks, backward)
            span(per, chunks, backward_end)
            unit_grad()

        drain(dpre_sib, ex_r.at[3])
        drain(normed_sib, ex_r.at[0])

        def in_quarter(q):
            own = jnp.concatenate([normed[q * blocks + i] for i in range(blocks)], axis=-1)
            other = jnp.concatenate([normed_sib[q * blocks + i] for i in range(blocks)], axis=-1)
            return tn(own, dpre[0]) + tn(other, dpre_sib[...])

        def in_send(i):
            side = 1 - 2 * lax.rem(i, 2)
            d2 = lax.rem(d + n_dp // 2 + side * lax.div(i + 1, 2), n_dp)
            xs_i[d2] = in_quarter(d2).astype(BF16)
            put(xs_i.at[d2], xr_i.at[d], dp_s.at[1], dp_r.at[1], {"dp": d2})

        over(n_dp - 1, in_send)
        gi_f[...] = in_quarter(d)

        drain(hidden_all.at[pl.ds(0, 2 * n_dp - 1)], ex_r.at[1])
        drain(dx_all.at[pl.ds(0, 2 * n_dp - 1)], ex_r.at[2])
        own_dx = jnp.concatenate([dxb[d * blocks + i] for i in range(blocks)], axis=-1)
        gout_o[...] = tn(hid[0], own_dx)

        def out_term(off):
            other = lax.rem(2 * d + c + off, 2 * n_dp)
            got = jnp.concatenate([dx_all[other, i] for i in range(blocks)], axis=-1)
            gout_o[...] += tn(hidden_all[other], got)

        span(1, 2 * n_dp, out_term)

        dp_out(gu_f[d], xr_u, 0, gun_o)
        drain(lrcv, rsem.at[G_LOSS, 0])
        loss_o[0] = jnp.max(lown[...] + lrcv[...]) * (1.0 / denom)
        dp_out(None, xr_i, 1, gin_o)

        drain(w_in, ssem.at[G_SIBW, 0])
        drain(w_out, ssem.at[G_SIBW, 1])
        drain(w_unit, ssem.at[G_LOSS, 1])
        drain(lown, ssem.at[G_LOSS, 0])
        drain(gu_sib, sib_s.at[0])
        drain(xs_u.at[pl.ds(0, n_dp - 1)], dp_s.at[0])
        drain(xs_i.at[pl.ds(0, n_dp - 1)], dp_s.at[1])
        drain(normed, ex_s.at[0])
        drain(hidden_all.at[pl.ds(0, 2 * n_dp - 1)], ex_s.at[1])
        drain(dx_all.at[pl.ds(0, 2 * n_dp - 1)], ex_s.at[2])
        drain(dpre_sib, ex_s.at[3])

        def finish(k):
            part_of = rsf.at[0, pl.ds(0, n_z - 1)]
            drain(part_of, ssem.at[G_FRS, k])
            drain(part_of, ssem.at[G_FINZ, k])

            drain(part_of, ssem.at[G_NRS, k])

            @pl.when(s != hub)
            def _():
                drain(ysend.at[k], ssem.at[G_NY, k])

            @pl.when(s == hub)
            def _():
                drain(rsf.at[0], ssem.at[G_NAG, k])

            @pl.when(s < last)
            def _():
                drain(rsf.at[0], ssem.at[G_FAG, k])

            @pl.when(s == last)
            def _():
                drain(osh.at[pl.ds(0, n_seg - 1)], ssem.at[G_FINY, k])

            @pl.when(s > 0)
            def _():
                drain(part_of, ssem.at[G_BRS, k])
                drain(rsf.at[0], ssem.at[G_BAG, k])

        def finish_micro(k):
            drain(stb.at[k, pl.ds(0, n_peer - 1)], ssem.at[G_STAT, k])

        over(chunks, finish)
        over(micros, finish_micro)

    vm = pltpu.VMEM
    lines = (n_z, all_rows, col)
    shard = (chunks, cut, col)
    scatter = (chunks, n_z, cut, col)
    scratch = [
        vm((width, hid_dev), BF16), vm((hid_dev, width), BF16), vm((voc_dev, width), BF16),
        vm((width, hid_dev), BF16), vm((hid_dev, width), BF16), vm((voc_dev, width), BF16),
        vm(lines, BF16), vm(lines, BF16), vm(lines, BF16),
        vm(scatter, BF16), vm(shard, BF16), vm((2, all_rows, hid_dev), BF16), vm((2, all_rows, hid_dev), F32),
        vm(lines, BF16), vm((all_rows, width), BF16),
        vm((micros, 2, voc_dev, rows), F32), vm((micros, 2, voc_dev, rows), F32),
        vm((micros, n_peer, 4, rows), F32), vm((2, micros, voc_dev, rows), BF16),
        vm(lines, BF16), vm(scatter, BF16), vm(shard, BF16),
        vm((chunks, n_seg - 1, cut, col), BF16), vm(lines, BF16), vm(shard, BF16),
        vm((2, all_rows, hid_dev), BF16), vm(lines, BF16), vm(scatter, BF16), vm(shard, BF16),
        vm(lines, BF16), vm((2 * n_dp, all_rows, hid_dev), BF16),
        vm((2 * n_dp, n_z // n_dp, all_rows, col), BF16), vm((all_rows, hid_dev), BF16),
        vm((n_dp, voc_dev, quarter), F32), vm((n_dp, voc_dev, quarter), BF16), vm((n_dp, voc_dev, quarter), BF16),
        vm((n_dp, voc_dev, quarter), BF16), vm((n_dp, voc_dev, quarter), BF16),
        vm((n_dp, quarter, hid_dev), BF16), vm((n_dp, quarter, hid_dev), BF16),
        vm((8, rows), F32), vm((8, 128), F32), vm((8, 128), F32),
        pltpu.SemaphoreType.DMA((N_GROUPS, chunks)), pltpu.SemaphoreType.DMA((N_GROUPS, chunks)),
        pltpu.SemaphoreType.DMA((1,)), pltpu.SemaphoreType.DMA((1,)),
        pltpu.SemaphoreType.DMA((2,)), pltpu.SemaphoreType.DMA((2,)),
        pltpu.SemaphoreType.DMA((4,)), pltpu.SemaphoreType.DMA((4,)),
    ]
    return kernel, scratch


def solution(mesh):
    n_seg, n_mp, n_dp = mesh.shape["segment"], mesh.shape["mp"], mesh.shape["dp"]

    def on_device(text_rows, durations, unit_targets, w_in, w_out, w_unit):
        micro, rows, width = text_rows.shape
        units = unit_targets.shape[1]
        hid_dev = w_in.shape[2]
        voc_dev = w_unit.shape[1]
        denom = float(micro * units * n_dp)
        kernel, scratch = make_kernel(
            n_seg, n_mp // 2, n_dp, micro // 2, 8, rows, width, hid_dev, voc_dev, units, denom
        )
        quarter = width // n_dp
        vmem = pl.BlockSpec(memory_space=pltpu.VMEM)
        hbm = pl.BlockSpec(memory_space=pl.ANY)
        loss, gin, gin_own, gout, gun = pl.pallas_call(
            kernel,
            out_shape=(
                jax.ShapeDtypeStruct((1,), F32),
                jax.ShapeDtypeStruct((quarter, hid_dev), F32),
                jax.ShapeDtypeStruct((quarter, hid_dev), F32),
                jax.ShapeDtypeStruct((hid_dev, quarter), F32),
                jax.ShapeDtypeStruct((voc_dev, quarter), F32),
            ),
            in_specs=[hbm, vmem, vmem, hbm, hbm, hbm],
            out_specs=(pl.BlockSpec(memory_space=pltpu.SMEM), vmem, vmem, vmem, vmem),
            scratch_shapes=scratch,
            compiler_params=pltpu.CompilerParams(
                collective_id=0, has_side_effects=True, vmem_limit_bytes=60 * 1024 * 1024
            ),
        )(
            text_rows, durations, unit_targets, w_in[0], w_out[0],
            jnp.transpose(w_unit),
        )
        return (loss, (gin + gin_own)[None], gout[None], jnp.transpose(gun))

    placed = (
        P(None, "dp", None),
        P(None, "dp", None),
        P(None, "dp"),
        P("segment", None, "mp"),
        P("segment", "mp", None),
        P(None, ("segment", "mp")),
    )
    return jax.shard_map(
        on_device,
        mesh=mesh,
        in_specs=placed,
        out_specs=(
            P("dp"),
            P("segment", "dp", "mp"),
            P("segment", "mp", "dp"),
            P("dp", ("segment", "mp")),
        ),
        check_vma=False,
    )
```
